32 devices in a mesh: band: 8 (over y, x, core), lev: 4 (over z).
Axes of the slice: x: 2, y: 2, z: 4, core: 2. Of those that a mesh axis runs over, the one named last changes fastest.
Arguments:
- spectral: bfloat16 [2, 2, 4, 1280, 2561], P(None, None, 'lev', 'band'), may hold values from -0.005859375 to 0.005859375
- legendre: bfloat16 [1280, 8, 2561], P('band'), may hold values from -6 to 6
- cycle_len: int32 [8], replicated, may hold values from 20 to 10256, as said below
- pair_wave: int32 [1280], replicated, may hold values from 0 to 1279, each once
- quad_weight: float32 [8], replicated, may hold values from 2 to 20
- forcing: bfloat16 [2, 4, 8, 10256], P(None, None, 'band', 'lev'), may hold values from -6 to 6
- mixing: bfloat16 [2, 4, 4], replicated, may hold values from -3 to 3
Outputs:
- tendency: bfloat16 [2, 2, 4, 1280, 2561], P(None, None, 'lev', 'band')
The draws below stay inside these ranges and needn't reach their ends.
Inputs may be any that keep to these rules, and one draw needn't show every extreme that they name: `cycle_len`: each length is 20 + 4 i for distinct cycle numbers i from 0 to 2559; the cycle of length 10256 is present in every draw. `pair_wave`: each number from 0 to 1279 appears once.
All inputs are finite; a program needn't handle non-finite values.
Results may differ from the reference program's by a relative error of at most 0.008.
Values may be sent and summed in bfloat16 or wider, within the bound.
A program may use at most 128 MiB of HBM per device.

```python
import math
import jax
import jax.numpy as jnp
from jax import lax

TRUNC = 2559
FIELDS = 2
PAIRS = 1280
PACK = 2561
CYCLES = 8
LEVELS = 4
SPAN = 2564
POINTS = 10256
N_BAND = 8
N_LEV = 4


def draw_cycle_len(key, part):
    order = jax.random.permutation(key, TRUNC).astype(jnp.int32)
    chosen = jnp.concatenate([order[:CYCLES - 1], jnp.full((1,), TRUNC, jnp.int32)])
    spots = jax.random.permutation(jax.random.fold_in(key, 7), CYCLES)
    chosen = chosen[spots]
    return (20 + 4 * chosen).astype(jnp.int32)


def level_of(stream_key, shape, shards, smallest, largest):
    def one(axis_at, shards_of):
        heights = jax.random.uniform(jax.random.fold_in(jax.random.fold_in(stream_key, 6), axis_at), (shards_of,), jnp.float32, smallest / len(shards), largest / len(shards))
        return jnp.repeat(jnp.exp(heights), shape[axis_at] // shards_of).reshape((-1,) + (1,) * (len(shape) - axis_at - 1))

    level = one(*shards[0])
    for cut in shards[1:]:
        level = level * one(*cut)
    return level


def bell_draw(own_key, dims, width, bound, pieces=(), held_as=jnp.bfloat16):
    loudness = level_of(own_key, dims, pieces, -0.22, 0.18) if pieces else 1.0
    array = jax.random.normal(own_key, dims, jnp.float32) * width * loudness
    return jnp.minimum(jnp.maximum(array, -bound), bound).astype(held_as)


def setup_inputs(seed: int = 0) -> dict:
    splits = jax.random.split(jax.random.key(seed), 8)
    spectral = bell_draw(splits[0], (2, FIELDS, LEVELS, PAIRS, PACK), (1.0 / (TRUNC + 1)), 0.005859375, ((2, 4), (3, 8)))
    legendre = bell_draw(splits[1], (PAIRS, CYCLES, PACK), 1.0, 6.0, ((0, 8),))
    cycle_len = draw_cycle_len(jax.random.fold_in(splits[7], 71), 0)
    pair_wave = jax.random.permutation(splits[3], PAIRS).astype(jnp.int32)
    quad_weight = jnp.clip(jnp.exp(jax.random.uniform(splits[4], (CYCLES,), jnp.float32, math.log(2.0), math.log(20.0))), 2.0, 20.0)
    forcing = bell_draw(splits[5], (FIELDS, LEVELS, CYCLES, POINTS), 1.0, 6.0, ((2, 8), (3, 4)))
    mixing = bell_draw(splits[6], (FIELDS, LEVELS, LEVELS), LEVELS ** -0.5, 3.0)
    return {"spectral": spectral, "legendre": legendre, "cycle_len": cycle_len, "pair_wave": pair_wave, "quad_weight": quad_weight, "forcing": forcing, "mixing": mixing}


TWO_PI = 6.283185307179586


def phases(numerator, length_value):
    residue = numerator % length_value
    angles = residue.astype(jnp.float32) * (TWO_PI / length_value.astype(jnp.float32))
    return jnp.cos(angles), jnp.sin(angles)


def lower_mask(lower_wave_list):
    column = jnp.arange(PACK, dtype=jnp.int32)
    return column[None, :] < (TRUNC + 1 - lower_wave_list)[:, None]


def reference(spectral, legendre, cycle_len, pair_wave, quad_weight, forcing, mixing):
    group_size = PAIRS // N_BAND
    spec_blocks = jnp.moveaxis(spectral.reshape(2, FIELDS, LEVELS, N_BAND, group_size, PACK), 3, 0)
    leg_blocks = legendre.reshape(N_BAND, group_size, CYCLES, PACK)
    low_blocks = pair_wave.reshape(N_BAND, group_size)

    def inverse_block(block_items):
        spec_blk, leg_blk, low_blk = block_items
        lower_part = lower_mask(low_blk)
        halves = jnp.stack([lower_part, jnp.logical_not(lower_part)], axis=1)
        masked = jnp.where(halves, spec_blk[:, :, :, :, None, :], jnp.zeros((), jnp.bfloat16))
        return jnp.einsum('rflphc,pjc->fljrph', masked.astype(jnp.float32), leg_blk.astype(jnp.float32))

    fourier = lax.map(inverse_block, (spec_blocks, leg_blocks, low_blocks))
    fourier = jnp.moveaxis(fourier, 0, 4).reshape(FIELDS, LEVELS, CYCLES, 2, TRUNC + 1)
    wave_list = jnp.stack([pair_wave, TRUNC - pair_wave], axis=1).reshape(-1)
    live_mask = 2 * wave_list[None, :] < cycle_len[:, None]
    fourier = jnp.where(live_mask[None, None, :, None, :], fourier, 0.0).astype(jnp.bfloat16)

    gauss_weight = jnp.where(wave_list == 0, 1.0, 2.0).astype(jnp.float32)
    points = jnp.arange(N_LEV, dtype=jnp.int32)[:, None] * SPAN + jnp.arange(SPAN, dtype=jnp.int32)[None, :]

    def cycle_tables(length_value):
        outer_num = wave_list[None, :] * (jnp.arange(N_LEV, dtype=jnp.int32) * SPAN)[:, None]
        outer_cos, outer_sin = phases(outer_num, length_value)
        inner_num = wave_list[:, None] * jnp.arange(SPAN, dtype=jnp.int32)[None, :]
        inner_cos, inner_sin = phases(inner_num, length_value)
        inner_table = jnp.concatenate([inner_cos, inner_sin], axis=0).astype(jnp.bfloat16)
        return outer_cos, outer_sin, inner_table

    def synthesize(block_items):
        coeffs, length_value = block_items
        outer_cos, outer_sin, inner_table = cycle_tables(length_value)
        part_re = coeffs[:, :, 0, None, :].astype(jnp.float32)
        part_im = coeffs[:, :, 1, None, :].astype(jnp.float32)
        twist_re = (gauss_weight * (part_re * outer_cos - part_im * outer_sin)).astype(jnp.bfloat16)
        twist_im = (gauss_weight * (part_re * outer_sin + part_im * outer_cos)).astype(jnp.bfloat16)
        stacked = jnp.concatenate([twist_re, -twist_im], axis=-1)
        grid_vals = jnp.einsum('flak,kb->flab', stacked.astype(jnp.float32), inner_table.astype(jnp.float32))
        return jnp.where((points < length_value)[None, None], grid_vals, 0.0)

    grid_vals = lax.map(synthesize, (jnp.moveaxis(fourier, 2, 0), cycle_len))
    grid_vals = jnp.moveaxis(grid_vals, 0, 2).reshape(FIELDS, LEVELS, CYCLES, POINTS)

    level_product = (grid_vals[0] * grid_vals[1]).astype(jnp.bfloat16)
    mixing_tendency = jnp.einsum('flm,mrp->flrp', mixing.astype(jnp.float32), level_product.astype(jnp.float32))
    summed = grid_vals + forcing.astype(jnp.float32) + mixing_tendency
    flat_points = jnp.arange(POINTS, dtype=jnp.int32)
    summed = jnp.where((flat_points[None, :] < cycle_len[:, None])[None, None], summed, 0.0)
    cycle_q = summed.astype(jnp.bfloat16)

    def analyse(block_items):
        values, length_value, cycle_weight = block_items
        outer_cos, outer_sin, inner_table = cycle_tables(length_value)
        blocks = values.reshape(FIELDS, LEVELS, N_LEV, SPAN).astype(jnp.float32)
        analysed = jnp.einsum('flab,kb->flak', blocks, inner_table.astype(jnp.float32))
        cos_part = analysed[..., :TRUNC + 1]
        sin_part = analysed[..., TRUNC + 1:]
        factor = cycle_weight / length_value.astype(jnp.float32)
        coeff_re = jnp.sum(cos_part * outer_cos - sin_part * outer_sin, axis=2) * factor
        coeff_im = -jnp.sum(cos_part * outer_sin + sin_part * outer_cos, axis=2) * factor
        keep_mask = 2 * wave_list < length_value
        coeff_re = jnp.where(keep_mask, coeff_re, 0.0)
        coeff_im = jnp.where(keep_mask, coeff_im, 0.0)
        return jnp.stack([coeff_re, coeff_im], axis=2).astype(jnp.bfloat16)

    spectral_in = lax.map(analyse, (jnp.moveaxis(cycle_q, 2, 0), cycle_len, quad_weight))
    spectral_in = spectral_in.reshape(CYCLES, FIELDS, LEVELS, 2, N_BAND, group_size, 2)
    spectral_in = jnp.moveaxis(spectral_in, 4, 0)

    def direct_block(block_items):
        coeff_blk, leg_blk, low_blk = block_items
        legendre_sum = jnp.einsum('jflrph,pjc->rflphc', coeff_blk.astype(jnp.float32), leg_blk.astype(jnp.float32))
        lower_part = lower_mask(low_blk)
        chosen = jnp.where(lower_part, legendre_sum[:, :, :, :, 0, :], legendre_sum[:, :, :, :, 1, :])
        return chosen.astype(jnp.bfloat16)

    result = lax.map(direct_block, (spectral_in, leg_blocks, low_blocks))
    return jnp.moveaxis(result, 0, 3).reshape(2, FIELDS, LEVELS, PAIRS, PACK)
```

```python
import functools

import jax
import jax.numpy as jnp
from jax import lax
from jax.experimental import pallas as pl
from jax.experimental.pallas import tpu as pltpu
from jax.sharding import PartitionSpec as P

TRUNC = 2559
FIELDS = 2
INNER = 256
VMEM_LIMIT = 32 << 20
TWO_PI = 6.283185307179586


def pair_block(pair_dev):
    return 16 if pair_dev % 16 == 0 else 8


def sincos(wave, point, length, inverse_length):
    number = wave * point
    turns = jnp.floor(number.astype(jnp.float32) * inverse_length).astype(jnp.int32)
    residue = (number - turns * length).astype(jnp.float32) * inverse_length
    quarter = jnp.floor(residue * 4.0 + 0.5)
    t = (residue - quarter * 0.25) * TWO_PI
    t2 = t * t
    sin_t = t * (1.0 + t2 * (-1.0 / 6 + t2 * (1.0 / 120 + t2 * (-1.0 / 5040 + t2 * (1.0 / 362880)))))
    cos_t = 1.0 + t2 * (
        -0.5 + t2 * (1.0 / 24 + t2 * (-1.0 / 720 + t2 * (1.0 / 40320 + t2 * (-1.0 / 3628800))))
    )
    q = quarter.astype(jnp.int32)
    swap = (q & 1) == 1
    cos_v = jnp.where(swap, sin_t, cos_t)
    sin_v = jnp.where(swap, cos_t, sin_t)
    cos_v = jnp.where(((q + 1) & 2) == 2, -cos_v, cos_v)
    sin_v = jnp.where((q & 2) == 2, -sin_v, sin_v)
    return cos_v, sin_v


def diagonal(pairs, cycles):
    rows = lax.broadcasted_iota(jnp.int32, (pairs, cycles, 8 * pairs), 0)
    lanes = lax.broadcasted_iota(jnp.int32, (pairs, cycles, 8 * pairs), 2) % pairs
    return rows == lanes


def toggled(index, flips, count):
    if count & (count - 1):
        return (index + flips) % count
    result, bit = 0, 1
    while bit < count:
        result = result + (index // bit + flips // bit) % 2 * bit
        bit *= 2
    return result


def direct_kernel(split, limit_ref, coeff_ref, leg_ref, out_hbm, out_vmem, out_sem):
    blocks, cycles, wide_lanes = coeff_ref.shape
    pairs = wide_lanes // 8
    packed = leg_ref.shape[2]

    def write(i):
        part = pl.ds(pl.multiple_of(i * pairs, pairs), pairs)
        return pltpu.make_async_copy(
            out_vmem.at[:, :, :, part], out_hbm.at[:, :, :, part], out_sem.at[i]
        )

    mask = diagonal(pairs, cycles)
    column = split + lax.broadcasted_iota(jnp.int32, (pairs, packed - split), 1)
    half = 4 * pairs

    @pl.loop(0, blocks)
    def _(i):
        part = pl.ds(pl.multiple_of(i * pairs, pairs), pairs)
        wide = jnp.broadcast_to(coeff_ref[pl.ds(i, 1)], (pairs, cycles, 8 * pairs))
        wide = jnp.where(mask, wide, 0.0).reshape(pairs * cycles, 8 * pairs)
        wide = wide.T.astype(jnp.bfloat16)
        lower = column < limit_ref[part]
        leg = leg_ref[part].reshape(pairs * cycles, packed)
        left = jnp.dot(wide[:half], leg[:, :split], preferred_element_type=jnp.float32)
        right = jnp.dot(wide, leg[:, split:], preferred_element_type=jnp.float32)
        for s in range(2):
            for f in range(FIELDS):
                at = (s * FIELDS + f) * pairs
                out_vmem[s, f, 0, part, :split] = left[at : at + pairs].astype(jnp.bfloat16)
                low, high = right[at : at + pairs], right[half + at : half + at + pairs]
                out_vmem[s, f, 0, part, split:] = jnp.where(lower, low, high).astype(jnp.bfloat16)
        write(i).start()

    for i in range(blocks):
        write(i).wait()


def grid_kernel(
    points_dev, levs, split, length_hbm, weight_hbm, low_hbm, forcing_hbm, mixing_hbm, spec_hbm, leg_hbm,
    out_ref, limit_ref, leg_ref,
    length_ref, weight_ref, low_ref, forcing_ref, mixing_ref,
    cos_tab, sin_tab, cos_out, sin_out, twist_re, twist_im, grid_ref,
    outgoing, incoming, partial, arrived, spec_vmem, four_ref, wave_ref,
    send_sem, recv_sem, send_back, recv_back, leg_sem, spec_sem, small_sem,
):
    blocks, cycles, wide = four_ref.shape
    pairs = wide // 8
    packed = leg_ref.shape[2]
    each = wide // 4

    def read_spec(i):
        part = pl.ds(pl.multiple_of(i * pairs, pairs), pairs)
        return pltpu.make_async_copy(
            spec_hbm.at[:, :, :, part], spec_vmem.at[:, :, :, part], spec_sem.at[i]
        )

    def read_leg(i):
        part = pl.ds(pl.multiple_of(i * pairs, pairs), pairs)
        return pltpu.make_async_copy(leg_hbm.at[part], leg_ref.at[part], leg_sem.at[i])

    small = [
        pltpu.make_async_copy(src, dst, small_sem.at[k])
        for k, (src, dst) in enumerate(
            (
                (low_hbm, low_ref), (length_hbm, length_ref), (weight_hbm, weight_ref),
                (forcing_hbm, forcing_ref), (mixing_hbm, mixing_ref),
            )
        )
    ]
    for copy in small[:3]:
        copy.start()
    for i in range(blocks):
        read_spec(i).start()
        read_leg(i).start()
    for copy in small[3:]:
        copy.start()

    rows = FIELDS * levs
    outer = cos_out.shape[0]
    used = pl.cdiv(points_dev, INNER)
    slots, _, lanes = incoming.shape
    bands = slots // levs
    band_id = lax.axis_index("band")
    lev_id = lax.axis_index("lev")
    me = band_id * levs + lev_id
    base = lev_id * points_dev
    barrier = pltpu.get_barrier_semaphore()

    def each_peer(act):
        def of_band(flips, skip):
            band = toggled(band_id, flips, bands)
            for turn in range(levs - 1, skip - 1, -1):
                act(band, (lev_id + turn) % levs)

        if slots <= 64:
            for flips in range(bands - 1, 0, -1):
                of_band(flips, 0)
        else:
            @pl.loop(1, bands)
            def _(step):
                of_band(bands - step, 0)
        of_band(0, 1)

    each_peer(
        lambda band, lev: pl.semaphore_signal(
            barrier, inc=1, device_id={"band": band, "lev": lev}, device_id_type=pl.DeviceIdType.MESH
        )
    )

    for copy in small[:3]:
        copy.wait()
    length = length_ref[band_id]
    inverse_length = 1.0 / jnp.full((1, lanes), length, jnp.int32).astype(jnp.float32)
    factor = inverse_length * weight_ref[band_id]

    own = blocks * pairs
    line = low_ref[...].reshape(1, bands * own)
    low = jnp.concatenate([line[:, k * own : (k + 1) * own] for k in range(bands)], axis=0)
    parts = [low, TRUNC - low]
    if lanes > blocks * each:
        parts.append(jnp.full((bands, lanes - blocks * each), 1 << 14, jnp.int32))
    wave_ref[...] = jnp.concatenate(parts, axis=1)
    mine = jnp.broadcast_to(wave_ref[pl.ds(band_id, 1), :].astype(jnp.float32), (8, lanes)).T
    limit_ref[...] = TRUNC + 1 - mine[: blocks * pairs, 0:1].astype(jnp.int32)

    def tables(c):
        span = pl.ds(pl.multiple_of(c * lanes, lanes), lanes)
        wave = wave_ref[pl.ds(c, 1), :]
        eight = lax.broadcasted_iota(jnp.int32, (8, lanes), 0)
        c0, s0 = sincos(wave, eight, length, inverse_length)
        c1, s1 = sincos(wave, eight * 8, length, inverse_length)
        c2, s2 = sincos(wave, eight * 64, length, inverse_length)
        steps = lax.broadcasted_iota(jnp.int32, (outer, lanes), 0)
        c3, s3 = sincos(wave, base + steps * INNER, length, inverse_length)
        cos_out[:, span] = c3
        sin_out[:, span] = s3
        for high in range(INNER // 64):
            ch, sh = c2[high : high + 1], s2[high : high + 1]
            cj, sj = ch * c1 - sh * s1, ch * s1 + sh * c1
            for mid in range(8):
                cm, sm = cj[mid : mid + 1], sj[mid : mid + 1]
                at = high * 64 + mid * 8
                cos_tab[at : at + 8, span] = (c0 * cm - s0 * sm).astype(jnp.bfloat16)
                sin_tab[at : at + 8, span] = (s0 * cm + c0 * sm).astype(jnp.bfloat16)

    mask = diagonal(pairs, cycles)
    column = split + lax.broadcasted_iota(jnp.int32, (pairs, packed - split), 1)
    inner = (((1,), (1,)), ((), ()))

    def legendre(i):
        part = pl.ds(pl.multiple_of(i * pairs, pairs), pairs)
        lower = column < limit_ref[part]
        whole, lows, highs = [], [], []
        for s in range(2):
            for f in range(FIELDS):
                whole.append(spec_vmem[s, f, 0, part, :split])
                row = spec_vmem[s, f, 0, part, split:].astype(jnp.float32)
                lows.append(jnp.where(lower, row, 0.0))
                highs.append(jnp.where(lower, 0.0, row))
        left = jnp.concatenate(whole, axis=0)
        right = jnp.concatenate(lows + highs, axis=0).astype(jnp.bfloat16)
        leg = leg_ref[part].reshape(pairs * cycles, packed)
        full = lax.dot_general(leg[:, split:], right, inner, preferred_element_type=jnp.float32)
        some = lax.dot_general(leg[:, :split], left, inner, preferred_element_type=jnp.float32)
        full = full + jnp.concatenate([some, jnp.zeros_like(some)], axis=1)
        full = full.reshape(pairs, cycles, 8 * pairs)
        four_ref[i] = jnp.sum(jnp.where(mask, full, 0.0), axis=0)

    def arrive(i):
        read_spec(i).wait()
        read_leg(i).wait()

    both = min(blocks, bands)
    @pl.loop(0, both)
    def _(i):
        arrive(i)
        legendre(i)
        tables(i)

    @pl.loop(both, blocks)
    def _(i):
        arrive(i)
        legendre(i)

    sides = []
    for k in range(4):
        parts = [
            four_ref[i, :, (4 * h + k) * pairs : (4 * h + k + 1) * pairs]
            for h in range(2)
            for i in range(blocks)
        ]
        if lanes > blocks * each:
            parts.append(jnp.zeros((cycles, lanes - blocks * each), jnp.float32))
        sides.append(jnp.concatenate(parts, axis=1))
    for j in range(cycles):
        block = jnp.concatenate([side[j : j + 1] for side in sides], axis=0)
        outgoing[j] = block.astype(jnp.bfloat16)

    pl.semaphore_wait(barrier, slots - 1)

    def send(source, target, here, there):
        def act(band, lev):
            pltpu.make_async_remote_copy(
                src_ref=source(band, lev), dst_ref=target.at[me], send_sem=here,
                recv_sem=there, device_id={"band": band, "lev": lev},
                device_id_type=pl.DeviceIdType.MESH,
            ).start()
        return act

    each_peer(send(lambda band, lev: outgoing.at[band], incoming, send_sem, recv_sem.at[band_id]))
    incoming[me] = outgoing[band_id]

    pl.loop(both, bands)(tables)

    def wait_all(semaphore, buffer, count):
        most = buffer.at[pl.ds(0, count)]
        pltpu.make_async_copy(most, most, semaphore).wait()

    contract = (((1,), (1,)), ((), ()))

    def synthesis(c, first):
        span = pl.ds(pl.multiple_of(c * lanes, lanes), lanes)
        wave = wave_ref[pl.ds(c, 1), :]
        gain = jnp.where(wave == 0, 1.0, 2.0)
        live = 2 * wave < length
        cells = [incoming[c * levs + lev].astype(jnp.float32) for lev in range(levs)]
        order = [(f, lev) for f in range(FIELDS) for lev in range(levs)]
        re = jnp.concatenate([cells[lev][f : f + 1] for f, lev in order], axis=0)
        im = jnp.concatenate([cells[lev][FIELDS + f : FIELDS + f + 1] for f, lev in order], axis=0)
        re = jnp.where(live, re * gain, 0.0)
        im = jnp.where(live, im * gain, 0.0)
        for a in range(used):
            co, so = cos_out[a : a + 1, span], sin_out[a : a + 1, span]
            twist_re[a * rows : (a + 1) * rows] = (re * co - im * so).astype(jnp.bfloat16)
            twist_im[a * rows : (a + 1) * rows] = -(re * so + im * co).astype(jnp.bfloat16)
        grid = lax.dot_general(
            twist_re[...], cos_tab[:, span], contract, preferred_element_type=jnp.float32
        ) + lax.dot_general(twist_im[...], sin_tab[:, span], contract, preferred_element_type=jnp.float32)
        grid_ref[...] = grid if first else grid_ref[...] + grid

    wait_all(recv_sem.at[band_id], incoming, levs - 1)
    synthesis(band_id, True)

    @pl.loop(1, bands)
    def _(flips):
        band = toggled(band_id, flips, bands)
        wait_all(recv_sem.at[band], incoming, levs)
        synthesis(band, False)

    for copy in small[3:]:
        copy.wait()
    lane = lax.broadcasted_iota(jnp.int32, (rows, INNER), 1)
    mixing = jnp.concatenate([mixing_ref[f].astype(jnp.float32) for f in range(FIELDS)], axis=0)
    updated = []
    for a in range(used):
        point = a * INNER + lane
        inside = (point < points_dev) & (base + point < length)
        cell = jnp.where(inside, grid_ref[a * rows : (a + 1) * rows], 0.0)
        product = (cell[:levs] * cell[levs:]).astype(jnp.bfloat16).astype(jnp.float32)
        span = slice(a * INNER, min((a + 1) * INNER, points_dev))
        force = jnp.concatenate([forcing_ref[f, :, span].astype(jnp.float32) for f in range(FIELDS)], axis=0)
        if force.shape[1] < INNER:
            rest = jnp.zeros((rows, INNER - force.shape[1]), jnp.float32)
            force = jnp.concatenate([force, rest], axis=1)
        total = cell + force
        for l2 in range(levs):
            total = total + mixing[:, l2 : l2 + 1] * product[l2 : l2 + 1]
        updated.append(jnp.where(inside, total, 0.0))
    updated = jnp.concatenate(updated, axis=0).astype(jnp.bfloat16)

    send_partial = send(
        lambda band, lev: partial.at[band * levs + lev], arrived, send_back, recv_back
    )

    def analysis(c):
        span = pl.ds(pl.multiple_of(c * lanes, lanes), lanes)
        cos_part = jnp.dot(updated, cos_tab[:, span], preferred_element_type=jnp.float32)
        sin_part = jnp.dot(updated, sin_tab[:, span], preferred_element_type=jnp.float32)
        re = jnp.zeros((rows, lanes), jnp.float32)
        im = jnp.zeros((rows, lanes), jnp.float32)
        for a in range(used):
            co, so = cos_out[a : a + 1, span], sin_out[a : a + 1, span]
            cp, sp = cos_part[a * rows : (a + 1) * rows], sin_part[a * rows : (a + 1) * rows]
            re = re + (cp * co - sp * so)
            im = im + (cp * so + sp * co)
        keep = 2 * wave_ref[pl.ds(c, 1), :] < length
        re = jnp.where(keep, re * factor, 0.0)
        im = jnp.where(keep, im * -factor, 0.0)
        for lev in range(levs):
            picks = [side[f * levs + lev : f * levs + lev + 1] for side in (re, im) for f in range(FIELDS)]
            partial[c * levs + lev] = jnp.concatenate(picks, axis=0).astype(jnp.bfloat16)

    def send_band(flips, skip):
        band = toggled(band_id, flips, bands)
        for turn in range(levs - 1, skip - 1, -1):
            send_partial(band, (lev_id + turn) % levs)

    analysis(toggled(band_id, bands - 1, bands))

    @pl.loop(1, bands)
    def _(step):
        analysis(toggled(band_id, bands - 1 - step, bands))
        send_band(bands - step, 0)

    arrived[me] = partial[me]
    send_band(0, 1)

    wait_all(recv_back, arrived, slots - 1)
    sums = []
    for j in range(cycles):
        total = arrived[j * levs].astype(jnp.float32)
        for lev in range(1, levs):
            total = total + arrived[j * levs + lev].astype(jnp.float32)
        sums.append(total)
    for k in range(4):
        side = jnp.concatenate([total[k : k + 1] for total in sums], axis=0)
        for h in range(2):
            for i in range(blocks):
                at, lane = (4 * h + k) * pairs, (h * blocks + i) * pairs
                out_ref[i, :, at : at + pairs] = side[:, lane : lane + pairs]
    wait_all(send_sem, incoming, slots - 1)
    wait_all(send_back, arrived, slots - 1)


def on_device(spectral, legendre, cycle_len, pair_wave, quad_weight, forcing, mixing):
    band_count = lax.axis_size("band")
    lev_count = lax.axis_size("lev")
    pair_dev = spectral.shape[3]
    cycles = legendre.shape[1]
    levels, points_dev = forcing.shape[1], forcing.shape[3]
    rows = FIELDS * levels
    pairs = pair_block(pair_dev)
    blocks = pair_dev // pairs

    each_band = pl.cdiv(2 * pair_dev, 128) * 128
    waves = band_count * each_band
    used = pl.cdiv(points_dev, INNER)
    outer = pl.cdiv(used, 8) * 8
    force = forcing.reshape(FIELDS, levels, points_dev)
    vmem = pl.BlockSpec(memory_space=pltpu.VMEM)
    slots = band_count * lev_count
    message = pltpu.VMEM((slots, 2 * FIELDS, each_band), jnp.bfloat16)
    split = (TRUNC + 2 - pair_wave.shape[0]) // 128 * 128
    hbm = pl.BlockSpec(memory_space=pltpu.HBM)
    coeff, limit, leg = pl.pallas_call(
        functools.partial(grid_kernel, points_dev, lev_count, split),
        in_specs=[hbm] * 7,
        out_specs=[vmem] * 3,
        out_shape=[
            pltpu.VMEM((blocks, cycles, 8 * pairs), jnp.float32),
            pltpu.VMEM((pair_dev, 1), jnp.int32),
            pltpu.VMEM(legendre.shape, jnp.bfloat16),
        ],
        scratch_shapes=[
            pltpu.SMEM(cycle_len.shape, jnp.int32),
            pltpu.SMEM(quad_weight.shape, jnp.float32),
            pltpu.VMEM(pair_wave.shape, jnp.int32),
            pltpu.VMEM(force.shape, jnp.bfloat16),
            pltpu.VMEM(mixing.shape, jnp.bfloat16),
            pltpu.VMEM((INNER, waves), jnp.bfloat16),
            pltpu.VMEM((INNER, waves), jnp.bfloat16),
            pltpu.VMEM((outer, waves), jnp.float32),
            pltpu.VMEM((outer, waves), jnp.float32),
            pltpu.VMEM((used * rows, each_band), jnp.bfloat16),
            pltpu.VMEM((used * rows, each_band), jnp.bfloat16),
            pltpu.VMEM((used * rows, INNER), jnp.float32),
            pltpu.VMEM((cycles, 2 * FIELDS, each_band), jnp.bfloat16),
            message, message, message,
            pltpu.VMEM(spectral.shape, jnp.bfloat16),
            pltpu.VMEM((blocks, cycles, 8 * pairs), jnp.float32),
            pltpu.VMEM((band_count, each_band), jnp.int32),
            pltpu.SemaphoreType.DMA,
            pltpu.SemaphoreType.DMA((band_count,)),
            pltpu.SemaphoreType.DMA,
            pltpu.SemaphoreType.DMA,
            pltpu.SemaphoreType.DMA((blocks,)),
            pltpu.SemaphoreType.DMA((blocks,)),
            pltpu.SemaphoreType.DMA((5,)),
        ],
        compiler_params=pltpu.CompilerParams(
            collective_id=0, has_side_effects=True, vmem_limit_bytes=VMEM_LIMIT
        ),
    )(
        *(
            pltpu.with_memory_space_constraint(array, pltpu.HBM)
            for array in (cycle_len, quad_weight, pair_wave, force, mixing, spectral, legendre)
        )
    )
    return pl.pallas_call(
        functools.partial(direct_kernel, split),
        in_specs=[vmem, vmem, vmem],
        out_specs=hbm,
        out_shape=jax.ShapeDtypeStruct(spectral.shape, jnp.bfloat16),
        scratch_shapes=[pltpu.VMEM(spectral.shape, jnp.bfloat16), pltpu.SemaphoreType.DMA((blocks,))],
        compiler_params=pltpu.CompilerParams(vmem_limit_bytes=VMEM_LIMIT),
    )(limit, coeff, leg)


def solution(mesh):
    return jax.shard_map(
        on_device,
        mesh=mesh,
        in_specs=(
            P(None, None, "lev", "band", None),
            P("band", None, None),
            P(),
            P(),
            P(),
            P(None, None, "band", "lev"),
            P(),
        ),
        out_specs=P(None, None, "lev", "band", None),
        check_vma=False,
    )
```

```python
import functools

import jax
import jax.numpy as jnp
from jax import lax
from jax.experimental import pallas as pl
from jax.experimental.pallas import tpu as pltpu
from jax.sharding import PartitionSpec as P

TRUNC = 2559
FIELDS = 2
INNER = 256
VMEM_LIMIT = 32 << 20
TWO_PI = 6.283185307179586


def pair_block(pair_dev):
    return 16 if pair_dev % 16 == 0 else 8


def sincos(wave, point, length, inverse_length):
    number = wave * point
    turns = jnp.floor(number.astype(jnp.float32) * inverse_length).astype(jnp.int32)
    residue = (number - turns * length).astype(jnp.float32) * inverse_length
    quarter = jnp.floor(residue * 4.0 + 0.5)
    t = (residue - quarter * 0.25) * TWO_PI
    t2 = t * t
    sin_t = t * (1.0 + t2 * (-1.0 / 6 + t2 * (1.0 / 120 + t2 * (-1.0 / 5040 + t2 * (1.0 / 362880)))))
    cos_t = 1.0 + t2 * (
        -0.5 + t2 * (1.0 / 24 + t2 * (-1.0 / 720 + t2 * (1.0 / 40320 + t2 * (-1.0 / 3628800))))
    )
    q = quarter.astype(jnp.int32)
    swap = (q & 1) == 1
    cos_v = jnp.where(swap, sin_t, cos_t)
    sin_v = jnp.where(swap, cos_t, sin_t)
    cos_v = jnp.where(((q + 1) & 2) == 2, -cos_v, cos_v)
    sin_v = jnp.where((q & 2) == 2, -sin_v, sin_v)
    return cos_v, sin_v


def diagonal(pairs, cycles):
    rows = lax.broadcasted_iota(jnp.int32, (pairs, cycles, 8 * pairs), 0)
    lanes = lax.broadcasted_iota(jnp.int32, (pairs, cycles, 8 * pairs), 2) % pairs
    return rows == lanes


def toggled(index, flips, count):
    if count & (count - 1):
        return (index + flips) % count
    result, bit = 0, 1
    while bit < count:
        result = result + (index // bit + flips // bit) % 2 * bit
        bit *= 2
    return result


def direct_kernel(split, limit_ref, coeff_ref, leg_ref, out_hbm, out_vmem, out_sem):
    blocks, cycles, wide_lanes = coeff_ref.shape
    pairs = wide_lanes // 8
    packed = leg_ref.shape[2]

    def write(i):
        part = pl.ds(pl.multiple_of(i * pairs, pairs), pairs)
        return pltpu.make_async_copy(
            out_vmem.at[:, :, :, part], out_hbm.at[:, :, :, part], out_sem.at[i]
        )

    mask = diagonal(pairs, cycles)
    column = split + lax.broadcasted_iota(jnp.int32, (pairs, packed - split), 1)
    half = 4 * pairs

    @pl.loop(0, blocks, unroll=blocks <= 10)
    def _(i):
        part = pl.ds(pl.multiple_of(i * pairs, pairs), pairs)
        wide = jnp.broadcast_to(coeff_ref[pl.ds(i, 1)], (pairs, cycles, 8 * pairs))
        wide = jnp.where(mask, wide, 0.0).reshape(pairs * cycles, 8 * pairs)
        wide = wide.T.astype(jnp.bfloat16)
        lower = column < limit_ref[part]
        leg = leg_ref[part].reshape(pairs * cycles, packed)
        left = jnp.dot(wide[:half], leg[:, :split], preferred_element_type=jnp.float32)
        right = jnp.dot(wide, leg[:, split:], preferred_element_type=jnp.float32)
        for s in range(2):
            for f in range(FIELDS):
                at = (s * FIELDS + f) * pairs
                out_vmem[s, f, 0, part, :split] = left[at : at + pairs].astype(jnp.bfloat16)
                low, high = right[at : at + pairs], right[half + at : half + at + pairs]
                out_vmem[s, f, 0, part, split:] = jnp.where(lower, low, high).astype(jnp.bfloat16)
        write(i).start()

    for i in range(blocks):
        write(i).wait()


def grid_kernel(
    points_dev, levs, split, length_hbm, weight_hbm, low_hbm, forcing_hbm, mixing_hbm, spec_hbm, leg_hbm,
    out_ref, limit_ref, leg_ref,
    length_ref, weight_ref, low_ref, forcing_ref, mixing_ref,
    cos_tab, sin_tab, cos_out, sin_out, grid_ref,
    outgoing, incoming, partial, arrived, spec_vmem, four_ref, wave_ref,
    send_sem, recv_sem, send_back, recv_back, leg_sem, spec_sem, small_sem,
):
    blocks, cycles, wide = four_ref.shape
    pairs = wide // 8
    packed = leg_ref.shape[2]
    each = wide // 4

    def read_spec(i):
        part = pl.ds(pl.multiple_of(i * pairs, pairs), pairs)
        return pltpu.make_async_copy(
            spec_hbm.at[:, :, :, part], spec_vmem.at[:, :, :, part], spec_sem.at[i]
        )

    def read_leg(i):
        part = pl.ds(pl.multiple_of(i * pairs, pairs), pairs)
        return pltpu.make_async_copy(leg_hbm.at[part], leg_ref.at[part], leg_sem.at[i])

    small = [
        pltpu.make_async_copy(src, dst, small_sem.at[k])
        for k, (src, dst) in enumerate(
            (
                (low_hbm, low_ref), (length_hbm, length_ref), (weight_hbm, weight_ref),
                (forcing_hbm, forcing_ref), (mixing_hbm, mixing_ref),
            )
        )
    ]
    for copy in small[:3]:
        copy.start()

    rows = FIELDS * levs
    outer = cos_out.shape[0]
    used = pl.cdiv(points_dev, INNER)
    slots, _, lanes = incoming.shape
    bands = slots // levs
    band_id = lax.axis_index("band")
    lev_id = lax.axis_index("lev")
    me = band_id * levs + lev_id
    base = lev_id * points_dev
    barrier = pltpu.get_barrier_semaphore()

    def each_peer(act):
        def of_band(flips, skip):
            band = toggled(band_id, flips, bands)
            for turn in range(levs - 1, skip - 1, -1):
                act(band, (lev_id + turn) % levs)

        if slots <= 64:
            for flips in range(bands - 1, 0, -1):
                of_band(flips, 0)
        else:
            @pl.loop(1, bands)
            def _(step):
                of_band(bands - step, 0)
        of_band(0, 1)

    each_peer(
        lambda band, lev: pl.semaphore_signal(
            barrier, inc=1, device_id={"band": band, "lev": lev}, device_id_type=pl.DeviceIdType.MESH
        )
    )

    for i in range(blocks):
        read_spec(i).start()
        read_leg(i).start()
    for copy in small[3:]:
        copy.start()

    for at, copy in enumerate(small[:3]):
        copy.wait()
    length = length_ref[band_id]
    inverse_length = 1.0 / jnp.full((1, lanes), length, jnp.int32).astype(jnp.float32)
    factor = inverse_length * weight_ref[band_id]

    own = blocks * pairs
    line = low_ref[...].reshape(1, bands * own)
    low = jnp.concatenate([line[:, k * own : (k + 1) * own] for k in range(bands)], axis=0)
    parts = [low, TRUNC - low]
    if lanes > blocks * each:
        parts.append(jnp.full((bands, lanes - blocks * each), 1 << 14, jnp.int32))
    wave_ref[...] = jnp.concatenate(parts, axis=1)
    mine = jnp.broadcast_to(wave_ref[pl.ds(band_id, 1), :].astype(jnp.float32), (8, lanes)).T
    limit_ref[...] = TRUNC + 1 - mine[: blocks * pairs, 0:1].astype(jnp.int32)

    def tables(c):
        span = pl.ds(pl.multiple_of(c * lanes, lanes), lanes)
        wave = wave_ref[pl.ds(c, 1), :]
        eight = lax.broadcasted_iota(jnp.int32, (8, lanes), 0)
        c0, s0 = sincos(wave, eight, length, inverse_length)
        c1, s1 = sincos(wave, eight * 8, length, inverse_length)
        c2, s2 = sincos(wave, eight * 64, length, inverse_length)
        steps = lax.broadcasted_iota(jnp.int32, (outer, lanes), 0)
        c3, s3 = sincos(wave, base + steps * INNER, length, inverse_length)
        cos_out[:, span] = c3
        sin_out[:, span] = s3
        for high in range(INNER // 64):
            ch, sh = c2[high : high + 1], s2[high : high + 1]
            cj, sj = ch * c1 - sh * s1, ch * s1 + sh * c1
            for mid in range(8):
                cm, sm = cj[mid : mid + 1], sj[mid : mid + 1]
                at = high * 64 + mid * 8
                cos_tab[at : at + 8, span] = (c0 * cm - s0 * sm).astype(jnp.bfloat16)
                sin_tab[at : at + 8, span] = (s0 * cm + c0 * sm).astype(jnp.bfloat16)

    mask = diagonal(pairs, cycles)
    column = split + lax.broadcasted_iota(jnp.int32, (pairs, packed - split), 1)
    inner = (((1,), (1,)), ((), ()))

    def legendre(i):
        part = pl.ds(pl.multiple_of(i * pairs, pairs), pairs)
        lower = column < limit_ref[part]
        whole, lows, highs = [], [], []
        for s in range(2):
            for f in range(FIELDS):
                whole.append(spec_vmem[s, f, 0, part, :split])
                row = spec_vmem[s, f, 0, part, split:].astype(jnp.float32)
                lows.append(jnp.where(lower, row, 0.0))
                highs.append(jnp.where(lower, 0.0, row))
        left = jnp.concatenate(whole, axis=0)
        right = jnp.concatenate(lows + highs, axis=0).astype(jnp.bfloat16)
        leg = leg_ref[part].reshape(pairs * cycles, packed)
        full = lax.dot_general(leg[:, split:], right, inner, preferred_element_type=jnp.float32)
        some = lax.dot_general(leg[:, :split], left, inner, preferred_element_type=jnp.float32)
        full = full + jnp.concatenate([some, jnp.zeros_like(some)], axis=1)
        full = full.reshape(pairs, cycles, 8 * pairs)
        four_ref[i] = jnp.sum(jnp.where(mask, full, 0.0), axis=0)

    def arrive(i):
        read_spec(i).wait()
        read_leg(i).wait()

    group = 2 if blocks % 2 == 0 else 1
    early = min(2, bands)

    pl.loop(0, early)(tables)

    @pl.loop(0, blocks // group)
    def _(step):
        first = step * group
        for at in range(group):
            arrive(first + at)
        for at in range(group):
            legendre(first + at)

    sides = []
    for k in range(4):
        parts = [
            four_ref[i, :, (4 * h + k) * pairs : (4 * h + k + 1) * pairs]
            for h in range(2)
            for i in range(blocks)
        ]
        if lanes > blocks * each:
            parts.append(jnp.zeros((cycles, lanes - blocks * each), jnp.float32))
        sides.append(jnp.concatenate(parts, axis=1))
    for j in range(cycles):
        block = jnp.concatenate([side[j : j + 1] for side in sides], axis=0)
        outgoing[j] = block.astype(jnp.bfloat16)

    pl.semaphore_wait(barrier, slots - 1)

    def send(source, target, here, there):
        def act(band, lev):
            pltpu.make_async_remote_copy(
                src_ref=source(band, lev), dst_ref=target.at[me], send_sem=here,
                recv_sem=there, device_id={"band": band, "lev": lev},
                device_id_type=pl.DeviceIdType.MESH,
            ).start()
        return act

    each_peer(send(lambda band, lev: outgoing.at[band], incoming, send_sem, recv_sem.at[band_id]))
    incoming[me] = outgoing[band_id]

    pl.loop(early, bands)(tables)

    def wait_all(semaphore, buffer, count):
        most = buffer.at[pl.ds(0, count)]
        pltpu.make_async_copy(most, most, semaphore).wait()

    contract = (((1,), (1,)), ((), ()))
    near = 2 if bands % 2 == 0 else 1
    groups = bands // near

    def span_of(group):
        return pl.ds(pl.multiple_of(group * (near * lanes), near * lanes), near * lanes)

    def waves_of(group):
        return jnp.concatenate([wave_ref[pl.ds(group * near + at, 1), :] for at in range(near)], axis=1)

    def synthesis(group):
        span, wave = span_of(group), waves_of(group)
        gain = jnp.where(wave == 0, 1.0, 2.0)
        live = 2 * wave < length
        cells = [
            jnp.concatenate([incoming[(group * near + at) * levs + lev] for at in range(near)], axis=1)
            for lev in range(levs)
        ]
        cells = [cell.astype(jnp.float32) for cell in cells]
        order = [(f, lev) for f in range(FIELDS) for lev in range(levs)]
        re = jnp.concatenate([cells[lev][f : f + 1] for f, lev in order], axis=0)
        im = jnp.concatenate([cells[lev][FIELDS + f : FIELDS + f + 1] for f, lev in order], axis=0)
        re = jnp.where(live, re * gain, 0.0)
        im = jnp.where(live, im * gain, 0.0)
        twist_re, twist_im = [], []
        for a in range(used):
            co, so = cos_out[a : a + 1, span], sin_out[a : a + 1, span]
            twist_re.append(re * co - im * so)
            twist_im.append(-(re * so + im * co))
        twist_re = jnp.concatenate(twist_re, axis=0).astype(jnp.bfloat16)
        twist_im = jnp.concatenate(twist_im, axis=0).astype(jnp.bfloat16)
        return lax.dot_general(
            twist_re, cos_tab[:, span], contract, preferred_element_type=jnp.float32
        ) + lax.dot_general(twist_im, sin_tab[:, span], contract, preferred_element_type=jnp.float32)

    def wait_group(flips, own):
        group = toggled(band_id // near, flips, groups)
        for at in range(near):
            if own:
                first = (band_id + at) % near
                wait_all(recv_sem.at[group * near + first], incoming, levs - (at == 0))
            else:
                wait_all(recv_sem.at[group * near + at], incoming, levs)
        return group

    if groups <= 8:
        these = [wait_group(flips, flips == 0) for flips in range(groups)]
        grid = sum(synthesis(group) for group in these)
    else:
        grid_ref[...] = synthesis(wait_group(0, True))

        @pl.loop(1, groups)
        def _(flips):
            grid_ref[...] += synthesis(wait_group(flips, False))

        grid = grid_ref[...]

    for copy in small[3:]:
        copy.wait()
    lane = lax.broadcasted_iota(jnp.int32, (rows, INNER), 1)
    mixing = jnp.concatenate([mixing_ref[f].astype(jnp.float32) for f in range(FIELDS)], axis=0)
    updated = []
    for a in range(used):
        point = a * INNER + lane
        inside = (point < points_dev) & (base + point < length)
        cell = jnp.where(inside, grid[a * rows : (a + 1) * rows], 0.0)
        product = (cell[:levs] * cell[levs:]).astype(jnp.bfloat16).astype(jnp.float32)
        span = slice(a * INNER, min((a + 1) * INNER, points_dev))
        force = jnp.concatenate([forcing_ref[f, :, span].astype(jnp.float32) for f in range(FIELDS)], axis=0)
        if force.shape[1] < INNER:
            rest = jnp.zeros((rows, INNER - force.shape[1]), jnp.float32)
            force = jnp.concatenate([force, rest], axis=1)
        total = cell + force
        for l2 in range(levs):
            total = total + mixing[:, l2 : l2 + 1] * product[l2 : l2 + 1]
        updated.append(jnp.where(inside, total, 0.0))
    updated = jnp.concatenate(updated, axis=0).astype(jnp.bfloat16)

    send_partial = send(
        lambda band, lev: partial.at[band * levs + lev], arrived, send_back, recv_back
    )

    def analysis(flips):
        group = toggled(band_id // near, flips, groups)
        span = span_of(group)
        cos_part = jnp.dot(updated, cos_tab[:, span], preferred_element_type=jnp.float32)
        sin_part = jnp.dot(updated, sin_tab[:, span], preferred_element_type=jnp.float32)
        re = jnp.zeros((rows, near * lanes), jnp.float32)
        im = jnp.zeros((rows, near * lanes), jnp.float32)
        for a in range(used):
            co, so = cos_out[a : a + 1, span], sin_out[a : a + 1, span]
            cp, sp = cos_part[a * rows : (a + 1) * rows], sin_part[a * rows : (a + 1) * rows]
            re = re + (cp * co - sp * so)
            im = im + (cp * so + sp * co)
        scale = jnp.concatenate([factor] * near, axis=1)
        keep = 2 * waves_of(group) < length
        re = jnp.where(keep, re * scale, 0.0)
        im = jnp.where(keep, im * -scale, 0.0)
        for lev in range(levs):
            picks = [side[f * levs + lev : f * levs + lev + 1] for side in (re, im) for f in range(FIELDS)]
            picks = jnp.concatenate(picks, axis=0).astype(jnp.bfloat16)
            for at in range(near):
                partial[(group * near + at) * levs + lev] = picks[:, at * lanes : (at + 1) * lanes]

    def send_group(flips):
        group = toggled(band_id // near, flips, groups)
        for at in range(near - 1, -1, -1):
            own = isinstance(flips, int) and flips == 0 and at == 0
            band = group * near + (band_id + at) % near
            for turn in range(levs - 1, 0 if own else -1, -1):
                send_partial(band, (lev_id + turn) % levs)

    analysis(groups - 1)
    if groups <= 8:
        for flips in range(groups - 2, -1, -1):
            analysis(flips)
            send_group(flips + 1)
    else:
        @pl.loop(1, groups)
        def _(step):
            analysis(groups - 1 - step)
            send_group(groups - step)

    arrived[me] = partial[me]
    send_group(0)

    wait_all(recv_back, arrived, slots - 1)
    sums = []
    for j in range(cycles):
        total = arrived[j * levs].astype(jnp.float32)
        for lev in range(1, levs):
            total = total + arrived[j * levs + lev].astype(jnp.float32)
        sums.append(total)
    for k in range(4):
        side = jnp.concatenate([total[k : k + 1] for total in sums], axis=0)
        for h in range(2):
            for i in range(blocks):
                at, lane = (4 * h + k) * pairs, (h * blocks + i) * pairs
                out_ref[i, :, at : at + pairs] = side[:, lane : lane + pairs]
    wait_all(send_sem, incoming, slots - 1)
    wait_all(send_back, arrived, slots - 1)


def on_device(spectral, legendre, cycle_len, pair_wave, quad_weight, forcing, mixing):
    band_count = lax.axis_size("band")
    lev_count = lax.axis_size("lev")
    pair_dev = spectral.shape[3]
    cycles = legendre.shape[1]
    levels, points_dev = forcing.shape[1], forcing.shape[3]
    rows = FIELDS * levels
    pairs = pair_block(pair_dev)
    blocks = pair_dev // pairs

    each_band = pl.cdiv(2 * pair_dev, 128) * 128
    waves = band_count * each_band
    used = pl.cdiv(points_dev, INNER)
    outer = pl.cdiv(used, 8) * 8
    force = forcing.reshape(FIELDS, levels, points_dev)
    vmem = pl.BlockSpec(memory_space=pltpu.VMEM)
    slots = band_count * lev_count
    message = pltpu.VMEM((slots, 2 * FIELDS, each_band), jnp.bfloat16)
    split = (TRUNC + 2 - pair_wave.shape[0]) // 128 * 128
    hbm = pl.BlockSpec(memory_space=pltpu.HBM)
    coeff, limit, leg = pl.pallas_call(
        functools.partial(grid_kernel, points_dev, lev_count, split),
        in_specs=[hbm] * 7,
        out_specs=[vmem] * 3,
        out_shape=[
            pltpu.VMEM((blocks, cycles, 8 * pairs), jnp.float32),
            pltpu.VMEM((pair_dev, 1), jnp.int32),
            pltpu.VMEM(legendre.shape, jnp.bfloat16),
        ],
        scratch_shapes=[
            pltpu.SMEM(cycle_len.shape, jnp.int32),
            pltpu.SMEM(quad_weight.shape, jnp.float32),
            pltpu.VMEM(pair_wave.shape, jnp.int32),
            pltpu.VMEM(force.shape, jnp.bfloat16),
            pltpu.VMEM(mixing.shape, jnp.bfloat16),
            pltpu.VMEM((INNER, waves), jnp.bfloat16),
            pltpu.VMEM((INNER, waves), jnp.bfloat16),
            pltpu.VMEM((outer, waves), jnp.float32),
            pltpu.VMEM((outer, waves), jnp.float32),
            pltpu.VMEM((used * rows, INNER), jnp.float32),
            pltpu.VMEM((cycles, 2 * FIELDS, each_band), jnp.bfloat16),
            message, message, message,
            pltpu.VMEM(spectral.shape, jnp.bfloat16),
            pltpu.VMEM((blocks, cycles, 8 * pairs), jnp.float32),
            pltpu.VMEM((band_count, each_band), jnp.int32),
            pltpu.SemaphoreType.DMA,
            pltpu.SemaphoreType.DMA((band_count,)),
            pltpu.SemaphoreType.DMA,
            pltpu.SemaphoreType.DMA,
            pltpu.SemaphoreType.DMA((blocks,)),
            pltpu.SemaphoreType.DMA((blocks,)),
            pltpu.SemaphoreType.DMA((5,)),
        ],
        compiler_params=pltpu.CompilerParams(
            collective_id=0, has_side_effects=True, vmem_limit_bytes=VMEM_LIMIT
        ),
    )(
        *(
            pltpu.with_memory_space_constraint(array, pltpu.HBM)
            for array in (cycle_len, quad_weight, pair_wave, force, mixing, spectral, legendre)
        )
    )
    return pl.pallas_call(
        functools.partial(direct_kernel, split),
        in_specs=[vmem, vmem, vmem],
        out_specs=hbm,
        out_shape=jax.ShapeDtypeStruct(spectral.shape, jnp.bfloat16),
        scratch_shapes=[pltpu.VMEM(spectral.shape, jnp.bfloat16), pltpu.SemaphoreType.DMA((blocks,))],
        compiler_params=pltpu.CompilerParams(vmem_limit_bytes=VMEM_LIMIT),
    )(limit, coeff, leg)


def solution(mesh):
    return jax.shard_map(
        on_device,
        mesh=mesh,
        in_specs=(
            P(None, None, "lev", "band", None),
            P("band", None, None),
            P(),
            P(),
            P(),
            P(None, None, "band", "lev"),
            P(),
        ),
        out_specs=P(None, None, "lev", "band", None),
        check_vma=False,
    )
```

```python
import functools

import jax
import jax.numpy as jnp
from jax import lax
from jax.experimental import pallas as pl
from jax.experimental.pallas import tpu as pltpu
from jax.sharding import PartitionSpec as P

TRUNC = 2559
FIELDS = 2
HALF = 128
INNER = 2 * HALF
VMEM_LIMIT = 32 << 20
TWO_PI = 6.283185307179586


def pair_block(pair_dev):
    return 16 if pair_dev % 16 == 0 else 8


def sincos(wave, point, length, inverse_length):
    number = wave * point
    turns = jnp.floor(number.astype(jnp.float32) * inverse_length).astype(jnp.int32)
    residue = (number - turns * length).astype(jnp.float32) * inverse_length
    quarter = jnp.floor(residue * 4.0 + 0.5)
    t = (residue - quarter * 0.25) * TWO_PI
    t2 = t * t
    sin_t = t * (1.0 + t2 * (-1.0 / 6 + t2 * (1.0 / 120 + t2 * (-1.0 / 5040 + t2 * (1.0 / 362880)))))
    cos_t = 1.0 + t2 * (
        -0.5 + t2 * (1.0 / 24 + t2 * (-1.0 / 720 + t2 * (1.0 / 40320 + t2 * (-1.0 / 3628800))))
    )
    q = quarter.astype(jnp.int32)
    swap = (q & 1) == 1
    cos_v = jnp.where(swap, sin_t, cos_t)
    sin_v = jnp.where(swap, cos_t, sin_t)
    cos_v = jnp.where(((q + 1) & 2) == 2, -cos_v, cos_v)
    sin_v = jnp.where((q & 2) == 2, -sin_v, sin_v)
    return cos_v, sin_v


def diagonal(pairs, cycles):
    rows = lax.broadcasted_iota(jnp.int32, (pairs, cycles, 8 * pairs), 0)
    lanes = lax.broadcasted_iota(jnp.int32, (pairs, cycles, 8 * pairs), 2) % pairs
    return rows == lanes


def toggled(index, flips, count):
    if count & (count - 1):
        return (index + flips) % count
    result, bit = 0, 1
    while bit < count:
        result = result + (index // bit + flips // bit) % 2 * bit
        bit *= 2
    return result


def direct_kernel(split, limit_ref, coeff_ref, leg_ref, out_hbm, out_vmem, out_sem):
    blocks, cycles, wide_lanes = coeff_ref.shape
    pairs = wide_lanes // 8
    packed = leg_ref.shape[2]

    def write(i):
        part = pl.ds(pl.multiple_of(i * pairs, pairs), pairs)
        return pltpu.make_async_copy(
            out_vmem.at[:, :, :, part], out_hbm.at[:, :, :, part], out_sem.at[i]
        )

    mask = diagonal(pairs, cycles)
    column = split + lax.broadcasted_iota(jnp.int32, (pairs, packed - split), 1)
    half = 4 * pairs

    @pl.loop(0, blocks, unroll=blocks <= 10)
    def _(i):
        part = pl.ds(pl.multiple_of(i * pairs, pairs), pairs)
        wide = jnp.broadcast_to(coeff_ref[pl.ds(i, 1)], (pairs, cycles, 8 * pairs))
        wide = jnp.where(mask, wide, 0.0).reshape(pairs * cycles, 8 * pairs)
        wide = wide.T.astype(jnp.bfloat16)
        lower = column < limit_ref[part]
        leg = leg_ref[part].reshape(pairs * cycles, packed)
        left = jnp.dot(wide[:half], leg[:, :split], preferred_element_type=jnp.float32)
        right = jnp.dot(wide, leg[:, split:], preferred_element_type=jnp.float32)
        for s in range(2):
            for f in range(FIELDS):
                at = (s * FIELDS + f) * pairs
                out_vmem[s, f, 0, part, :split] = left[at : at + pairs].astype(jnp.bfloat16)
                low, high = right[at : at + pairs], right[half + at : half + at + pairs]
                out_vmem[s, f, 0, part, split:] = jnp.where(lower, low, high).astype(jnp.bfloat16)
        write(i).start()

    for i in range(blocks):
        write(i).wait()


def grid_kernel(
    points_dev, levs, split, length_hbm, weight_hbm, low_hbm, forcing_hbm, mixing_hbm, spec_hbm, leg_hbm,
    out_ref, limit_ref, leg_ref,
    length_ref, weight_ref, low_ref, forcing_ref, mixing_ref,
    cos_tab, sin_tab, cos_out, sin_out, grid_ref, force_ref,
    outgoing, incoming, partial, arrived, spec_vmem, four_ref, wave_ref,
    send_sem, recv_sem, send_back, recv_back, leg_sem, spec_sem, small_sem,
):
    blocks, cycles, wide = four_ref.shape
    pairs = wide // 8
    packed = leg_ref.shape[2]
    each = wide // 4

    def read_spec(i):
        part = pl.ds(pl.multiple_of(i * pairs, pairs), pairs)
        return pltpu.make_async_copy(
            spec_hbm.at[:, :, :, part], spec_vmem.at[:, :, :, part], spec_sem.at[i]
        )

    def read_leg(i):
        part = pl.ds(pl.multiple_of(i * pairs, pairs), pairs)
        return pltpu.make_async_copy(leg_hbm.at[part], leg_ref.at[part], leg_sem.at[i])

    small = [
        pltpu.make_async_copy(src, dst, small_sem.at[k])
        for k, (src, dst) in enumerate(
            (
                (low_hbm, low_ref), (length_hbm, length_ref), (weight_hbm, weight_ref),
                (forcing_hbm, forcing_ref), (mixing_hbm, mixing_ref),
            )
        )
    ]
    for copy in small[:3]:
        copy.start()

    rows = FIELDS * levs
    outer = cos_out.shape[0]
    used = pl.cdiv(points_dev, INNER)
    slots, _, lanes = incoming.shape
    bands = slots // levs
    band_id = lax.axis_index("band")
    lev_id = lax.axis_index("lev")
    me = band_id * levs + lev_id
    base = lev_id * points_dev
    barrier = pltpu.get_barrier_semaphore()

    def each_peer(act):
        def of_band(flips, skip):
            band = toggled(band_id, flips, bands)
            for turn in range(levs - 1, skip - 1, -1):
                act(band, (lev_id + turn) % levs)

        if slots <= 64:
            for flips in range(bands - 1, 0, -1):
                of_band(flips, 0)
        else:
            @pl.loop(1, bands)
            def _(step):
                of_band(bands - step, 0)
        of_band(0, 1)

    each_peer(
        lambda band, lev: pl.semaphore_signal(
            barrier, inc=1, device_id={"band": band, "lev": lev}, device_id_type=pl.DeviceIdType.MESH
        )
    )

    for i in range(blocks):
        read_spec(i).start()
        read_leg(i).start()
    for copy in small[3:]:
        copy.start()

    for at, copy in enumerate(small[:3]):
        copy.wait()
    length = length_ref[band_id]
    inverse_length = 1.0 / jnp.full((1, lanes), length, jnp.int32).astype(jnp.float32)
    factor = inverse_length * weight_ref[band_id]

    own = blocks * pairs
    line = low_ref[...].reshape(1, bands * own)
    low = jnp.concatenate([line[:, k * own : (k + 1) * own] for k in range(bands)], axis=0)
    parts = [low, TRUNC - low]
    if lanes > blocks * each:
        parts.append(jnp.full((bands, lanes - blocks * each), 1 << 14, jnp.int32))
    wave_ref[...] = jnp.concatenate(parts, axis=1)
    mine = jnp.broadcast_to(wave_ref[pl.ds(band_id, 1), :].astype(jnp.float32), (8, lanes)).T
    limit_ref[...] = TRUNC + 1 - mine[: blocks * pairs, 0:1].astype(jnp.int32)

    twice, inverse_twice = 2 * length, 0.5 * inverse_length

    def tables(c):
        span = pl.ds(pl.multiple_of(c * lanes, lanes), lanes)
        wave = wave_ref[pl.ds(c, 1), :]
        eight = lax.broadcasted_iota(jnp.int32, (8, lanes), 0)
        c0, s0 = sincos(wave, eight * 2 + 1, twice, inverse_twice)
        c1, s1 = sincos(wave, eight * 16, twice, inverse_twice)
        c2, s2 = sincos(wave, eight * 128, twice, inverse_twice)
        steps = lax.broadcasted_iota(jnp.int32, (outer, lanes), 0)
        c3, s3 = sincos(wave, 2 * base + INNER - 1 + steps * (2 * INNER), twice, inverse_twice)
        cos_out[:, span] = c3
        sin_out[:, span] = s3
        for high in range(HALF // 64):
            ch, sh = c2[high : high + 1], s2[high : high + 1]
            cj, sj = ch * c1 - sh * s1, ch * s1 + sh * c1
            for mid in range(8):
                cm, sm = cj[mid : mid + 1], sj[mid : mid + 1]
                at = high * 64 + mid * 8
                cos_tab[at : at + 8, span] = (c0 * cm - s0 * sm).astype(jnp.bfloat16)
                sin_tab[at : at + 8, span] = (s0 * cm + c0 * sm).astype(jnp.bfloat16)

    mask = diagonal(pairs, cycles)
    column = split + lax.broadcasted_iota(jnp.int32, (pairs, packed - split), 1)
    inner = (((1,), (1,)), ((), ()))

    def legendre(i):
        part = pl.ds(pl.multiple_of(i * pairs, pairs), pairs)
        lower = column < limit_ref[part]
        whole, lows, highs = [], [], []
        for s in range(2):
            for f in range(FIELDS):
                whole.append(spec_vmem[s, f, 0, part, :split])
                row = spec_vmem[s, f, 0, part, split:].astype(jnp.float32)
                lows.append(jnp.where(lower, row, 0.0))
                highs.append(jnp.where(lower, 0.0, row))
        left = jnp.concatenate(whole, axis=0)
        right = jnp.concatenate(lows + highs, axis=0).astype(jnp.bfloat16)
        leg = leg_ref[part].reshape(pairs * cycles, packed)
        full = lax.dot_general(leg[:, split:], right, inner, preferred_element_type=jnp.float32)
        some = lax.dot_general(leg[:, :split], left, inner, preferred_element_type=jnp.float32)
        full = full + jnp.concatenate([some, jnp.zeros_like(some)], axis=1)
        full = full.reshape(pairs, cycles, 8 * pairs)
        four_ref[i] = jnp.sum(jnp.where(mask, full, 0.0), axis=0)

    def arrive(i):
        read_spec(i).wait()
        read_leg(i).wait()

    group = 2 if blocks % 2 == 0 else 1
    early = min(2, bands)

    pl.loop(0, early)(tables)

    @pl.loop(0, blocks // group)
    def _(step):
        first = step * group
        for at in range(group):
            arrive(first + at)
        for at in range(group):
            legendre(first + at)

    sides = []
    for k in range(4):
        parts = [
            four_ref[i, :, (4 * h + k) * pairs : (4 * h + k + 1) * pairs]
            for h in range(2)
            for i in range(blocks)
        ]
        if lanes > blocks * each:
            parts.append(jnp.zeros((cycles, lanes - blocks * each), jnp.float32))
        sides.append(jnp.concatenate(parts, axis=1))
    for j in range(cycles):
        block = jnp.concatenate([side[j : j + 1] for side in sides], axis=0)
        outgoing[j] = block.astype(jnp.bfloat16)

    pl.semaphore_wait(barrier, slots - 1)

    def send(source, target, here, there):
        def act(band, lev):
            pltpu.make_async_remote_copy(
                src_ref=source(band, lev), dst_ref=target.at[me], send_sem=here,
                recv_sem=there, device_id={"band": band, "lev": lev},
                device_id_type=pl.DeviceIdType.MESH,
            ).start()
        return act

    each_peer(send(lambda band, lev: outgoing.at[band], incoming, send_sem, recv_sem.at[band_id]))
    incoming[me] = outgoing[band_id]

    pl.loop(early, bands)(tables)

    def force_at(start):
        stop = min(start + HALF, points_dev)
        if stop <= start:
            return jnp.zeros((rows, HALF), jnp.float32)
        force = [forcing_ref[f, :, start:stop].astype(jnp.float32) for f in range(FIELDS)]
        force = jnp.concatenate(force, axis=0)
        if stop < start + HALF:
            rest = jnp.zeros((rows, start + HALF - stop), jnp.float32)
            force = jnp.concatenate([force, rest], axis=1)
        return force

    for copy in small[3:]:
        copy.wait()
    before = jnp.concatenate([force_at(a * INNER) for a in range(used)], axis=0)
    turned = lax.broadcasted_iota(jnp.int32, (HALF, HALF), 0) + lax.broadcasted_iota(
        jnp.int32, (HALF, HALF), 1
    )
    turned = jnp.where(turned == HALF - 1, 1.0, 0.0).astype(jnp.bfloat16)
    force_ref[0] = jnp.concatenate([force_at(a * INNER + HALF) for a in range(used)], axis=0)
    force_ref[1] = jnp.dot(before.astype(jnp.bfloat16), turned, preferred_element_type=jnp.float32)

    def wait_all(semaphore, buffer, count):
        most = buffer.at[pl.ds(0, count)]
        pltpu.make_async_copy(most, most, semaphore).wait()

    contract = (((1,), (1,)), ((), ()))
    near = 2 if bands % 2 == 0 else 1
    groups = bands // near

    def span_of(group):
        return pl.ds(pl.multiple_of(group * (near * lanes), near * lanes), near * lanes)

    def waves_of(group):
        return jnp.concatenate([wave_ref[pl.ds(group * near + at, 1), :] for at in range(near)], axis=1)

    def synthesis(group):
        span, wave = span_of(group), waves_of(group)
        gain = jnp.where(wave == 0, 1.0, 2.0)
        live = 2 * wave < length
        cells = [
            jnp.concatenate([incoming[(group * near + at) * levs + lev] for at in range(near)], axis=1)
            for lev in range(levs)
        ]
        cells = [cell.astype(jnp.float32) for cell in cells]
        order = [(f, lev) for f in range(FIELDS) for lev in range(levs)]
        re = jnp.concatenate([cells[lev][f : f + 1] for f, lev in order], axis=0)
        im = jnp.concatenate([cells[lev][FIELDS + f : FIELDS + f + 1] for f, lev in order], axis=0)
        re = jnp.where(live, re * gain, 0.0)
        im = jnp.where(live, im * gain, 0.0)
        twist_re, twist_im = [], []
        for a in range(used):
            co, so = cos_out[a : a + 1, span], sin_out[a : a + 1, span]
            twist_re.append(re * co - im * so)
            twist_im.append(-(re * so + im * co))
        twist_re = jnp.concatenate(twist_re, axis=0).astype(jnp.bfloat16)
        twist_im = jnp.concatenate(twist_im, axis=0).astype(jnp.bfloat16)
        even = lax.dot_general(twist_re, cos_tab[:, span], contract, preferred_element_type=jnp.float32)
        odd = lax.dot_general(twist_im, sin_tab[:, span], contract, preferred_element_type=jnp.float32)
        return even, odd

    def wait_group(flips, own):
        group = toggled(band_id // near, flips, groups)
        for at in range(near):
            if own:
                first = (band_id + at) % near
                wait_all(recv_sem.at[group * near + first], incoming, levs - (at == 0))
            else:
                wait_all(recv_sem.at[group * near + at], incoming, levs)
        return group

    if groups <= 8:
        these = [wait_group(flips, flips == 0) for flips in range(groups)]
        halves = [synthesis(group) for group in these]
        even = sum(half[0] for half in halves)
        odd = sum(half[1] for half in halves)
    else:
        grid_ref[0], grid_ref[1] = synthesis(wait_group(0, True))

        @pl.loop(1, groups)
        def _(flips):
            half = synthesis(wait_group(flips, False))
            grid_ref[0] += half[0]
            grid_ref[1] += half[1]

        even, odd = grid_ref[0], grid_ref[1]

    lane = lax.broadcasted_iota(jnp.int32, (rows, HALF), 1)
    mixing = jnp.concatenate([mixing_ref[f].astype(jnp.float32) for f in range(FIELDS)], axis=0)

    def physics(side, values, a):
        point = a * INNER + (HALF - 1 - lane if side else HALF + lane)
        inside = (point < points_dev) & (base + point < length)
        cell = jnp.where(inside, values, 0.0)
        product = (cell[:levs] * cell[levs:]).astype(jnp.bfloat16).astype(jnp.float32)
        total = cell + force_ref[side, a * rows : (a + 1) * rows]
        for l2 in range(levs):
            total = total + mixing[:, l2 : l2 + 1] * product[l2 : l2 + 1]
        return jnp.where(inside, total, 0.0)

    sums, gaps = [], []
    for a in range(used):
        at = slice(a * rows, (a + 1) * rows)
        after, before = physics(0, even[at] + odd[at], a), physics(1, even[at] - odd[at], a)
        sums.append(after + before)
        gaps.append(after - before)
    sums = jnp.concatenate(sums, axis=0).astype(jnp.bfloat16)
    gaps = jnp.concatenate(gaps, axis=0).astype(jnp.bfloat16)

    send_partial = send(
        lambda band, lev: partial.at[band * levs + lev], arrived, send_back, recv_back
    )

    def analysis(flips):
        group = toggled(band_id // near, flips, groups)
        span = span_of(group)
        cos_part = jnp.dot(sums, cos_tab[:, span], preferred_element_type=jnp.float32)
        sin_part = jnp.dot(gaps, sin_tab[:, span], preferred_element_type=jnp.float32)
        re = jnp.zeros((rows, near * lanes), jnp.float32)
        im = jnp.zeros((rows, near * lanes), jnp.float32)
        for a in range(used):
            co, so = cos_out[a : a + 1, span], sin_out[a : a + 1, span]
            cp, sp = cos_part[a * rows : (a + 1) * rows], sin_part[a * rows : (a + 1) * rows]
            re = re + (cp * co - sp * so)
            im = im + (cp * so + sp * co)
        scale = jnp.concatenate([factor] * near, axis=1)
        keep = 2 * waves_of(group) < length
        re = jnp.where(keep, re * scale, 0.0)
        im = jnp.where(keep, im * -scale, 0.0)
        for lev in range(levs):
            picks = [side[f * levs + lev : f * levs + lev + 1] for side in (re, im) for f in range(FIELDS)]
            picks = jnp.concatenate(picks, axis=0).astype(jnp.bfloat16)
            for at in range(near):
                partial[(group * near + at) * levs + lev] = picks[:, at * lanes : (at + 1) * lanes]

    def send_group(flips):
        group = toggled(band_id // near, flips, groups)
        for at in range(near - 1, -1, -1):
            own = isinstance(flips, int) and flips == 0 and at == 0
            band = group * near + (band_id + at) % near
            for turn in range(levs - 1, 0 if own else -1, -1):
                send_partial(band, (lev_id + turn) % levs)

    analysis(groups - 1)
    if groups <= 8:
        for flips in range(groups - 2, -1, -1):
            analysis(flips)
            send_group(flips + 1)
    else:
        @pl.loop(1, groups)
        def _(step):
            analysis(groups - 1 - step)
            send_group(groups - step)

    arrived[me] = partial[me]
    send_group(0)

    wait_all(recv_back, arrived, slots - 1)
    levels_sum = []
    for j in range(cycles):
        total = arrived[j * levs].astype(jnp.float32)
        for lev in range(1, levs):
            total = total + arrived[j * levs + lev].astype(jnp.float32)
        levels_sum.append(total)
    for k in range(4):
        side = jnp.concatenate([total[k : k + 1] for total in levels_sum], axis=0)
        for h in range(2):
            for i in range(blocks):
                at, lane = (4 * h + k) * pairs, (h * blocks + i) * pairs
                out_ref[i, :, at : at + pairs] = side[:, lane : lane + pairs]
    wait_all(send_sem, incoming, slots - 1)
    wait_all(send_back, arrived, slots - 1)


def on_device(spectral, legendre, cycle_len, pair_wave, quad_weight, forcing, mixing):
    band_count = lax.axis_size("band")
    lev_count = lax.axis_size("lev")
    pair_dev = spectral.shape[3]
    cycles = legendre.shape[1]
    levels, points_dev = forcing.shape[1], forcing.shape[3]
    rows = FIELDS * levels
    pairs = pair_block(pair_dev)
    blocks = pair_dev // pairs

    each_band = pl.cdiv(2 * pair_dev, 128) * 128
    waves = band_count * each_band
    used = pl.cdiv(points_dev, INNER)
    outer = pl.cdiv(used, 8) * 8
    force = forcing.reshape(FIELDS, levels, points_dev)
    vmem = pl.BlockSpec(memory_space=pltpu.VMEM)
    slots = band_count * lev_count
    message = pltpu.VMEM((slots, 2 * FIELDS, each_band), jnp.bfloat16)
    split = (TRUNC + 2 - pair_wave.shape[0]) // 128 * 128
    hbm = pl.BlockSpec(memory_space=pltpu.HBM)
    coeff, limit, leg = pl.pallas_call(
        functools.partial(grid_kernel, points_dev, lev_count, split),
        in_specs=[hbm] * 7,
        out_specs=[vmem] * 3,
        out_shape=[
            pltpu.VMEM((blocks, cycles, 8 * pairs), jnp.float32),
            pltpu.VMEM((pair_dev, 1), jnp.int32),
            pltpu.VMEM(legendre.shape, jnp.bfloat16),
        ],
        scratch_shapes=[
            pltpu.SMEM(cycle_len.shape, jnp.int32),
            pltpu.SMEM(quad_weight.shape, jnp.float32),
            pltpu.VMEM(pair_wave.shape, jnp.int32),
            pltpu.VMEM(force.shape, jnp.bfloat16),
            pltpu.VMEM(mixing.shape, jnp.bfloat16),
            pltpu.VMEM((HALF, waves), jnp.bfloat16),
            pltpu.VMEM((HALF, waves), jnp.bfloat16),
            pltpu.VMEM((outer, waves), jnp.float32),
            pltpu.VMEM((outer, waves), jnp.float32),
            pltpu.VMEM((2, used * rows, HALF), jnp.float32),
            pltpu.VMEM((2, used * rows, HALF), jnp.float32),
            pltpu.VMEM((cycles, 2 * FIELDS, each_band), jnp.bfloat16),
            message, message, message,
            pltpu.VMEM(spectral.shape, jnp.bfloat16),
            pltpu.VMEM((blocks, cycles, 8 * pairs), jnp.float32),
            pltpu.VMEM((band_count, each_band), jnp.int32),
            pltpu.SemaphoreType.DMA,
            pltpu.SemaphoreType.DMA((band_count,)),
            pltpu.SemaphoreType.DMA,
            pltpu.SemaphoreType.DMA,
            pltpu.SemaphoreType.DMA((blocks,)),
            pltpu.SemaphoreType.DMA((blocks,)),
            pltpu.SemaphoreType.DMA((5,)),
        ],
        compiler_params=pltpu.CompilerParams(
            collective_id=0, has_side_effects=True, vmem_limit_bytes=VMEM_LIMIT
        ),
    )(
        *(
            pltpu.with_memory_space_constraint(array, pltpu.HBM)
            for array in (cycle_len, quad_weight, pair_wave, force, mixing, spectral, legendre)
        )
    )
    return pl.pallas_call(
        functools.partial(direct_kernel, split),
        in_specs=[vmem, vmem, vmem],
        out_specs=hbm,
        out_shape=jax.ShapeDtypeStruct(spectral.shape, jnp.bfloat16),
        scratch_shapes=[pltpu.VMEM(spectral.shape, jnp.bfloat16), pltpu.SemaphoreType.DMA((blocks,))],
        compiler_params=pltpu.CompilerParams(vmem_limit_bytes=VMEM_LIMIT),
    )(limit, coeff, leg)


def solution(mesh):
    return jax.shard_map(
        on_device,
        mesh=mesh,
        in_specs=(
            P(None, None, "lev", "band", None),
            P("band", None, None),
            P(),
            P(),
            P(),
            P(None, None, "band", "lev"),
            P(),
        ),
        out_specs=P(None, None, "lev", "band", None),
        check_vma=False,
    )
```

```python
import functools

import jax
import jax.numpy as jnp
from jax import lax
from jax.experimental import pallas as pl
from jax.experimental.pallas import tpu as pltpu
from jax.sharding import PartitionSpec as P

TRUNC = 2559
FIELDS = 2
HALF = 128
INNER = 2 * HALF
VMEM_LIMIT = 32 << 20
STEP = 2
CHUNK = 256
TWO_PI = 6.283185307179586


def pair_block(pair_dev):
    return 16 if pair_dev % 16 == 0 else 8


def sincos(wave, point, length, inverse_length):
    number = wave * point
    turns = jnp.floor(number.astype(jnp.float32) * inverse_length).astype(jnp.int32)
    residue = (number - turns * length).astype(jnp.float32) * inverse_length
    quarter = jnp.floor(residue * 4.0 + 0.5)
    t = (residue - quarter * 0.25) * TWO_PI
    t2 = t * t
    sin_t = t * (1.0 + t2 * (-1.0 / 6 + t2 * (1.0 / 120 + t2 * (-1.0 / 5040 + t2 * (1.0 / 362880)))))
    cos_t = 1.0 + t2 * (
        -0.5 + t2 * (1.0 / 24 + t2 * (-1.0 / 720 + t2 * (1.0 / 40320 + t2 * (-1.0 / 3628800))))
    )
    q = quarter.astype(jnp.int32)
    swap = (q & 1) == 1
    cos_v = jnp.where(swap, sin_t, cos_t)
    sin_v = jnp.where(swap, cos_t, sin_t)
    cos_v = jnp.where(((q + 1) & 2) == 2, -cos_v, cos_v)
    sin_v = jnp.where((q & 2) == 2, -sin_v, sin_v)
    return cos_v, sin_v


def diagonal(pairs, cycles):
    rows = lax.broadcasted_iota(jnp.int32, (pairs, cycles, 8 * pairs), 0)
    lanes = lax.broadcasted_iota(jnp.int32, (pairs, cycles, 8 * pairs), 2) % pairs
    return rows == lanes


def toggled(index, flips, count):
    if count & (count - 1):
        return (index + flips) % count
    result, bit = 0, 1
    while bit < count:
        result = result + (index // bit + flips // bit) % 2 * bit
        bit *= 2
    return result


def direct_kernel(split, limit_ref, coeff_ref, leg_ref, out_hbm, out_vmem, out_sem):
    blocks, cycles, wide_lanes = coeff_ref.shape
    pairs = wide_lanes // 8
    packed = leg_ref.shape[2]

    def write(i):
        part = pl.ds(pl.multiple_of(i * pairs, pairs), pairs)
        return pltpu.make_async_copy(
            out_vmem.at[:, :, :, part], out_hbm.at[:, :, :, part], out_sem.at[i]
        )

    mask = diagonal(pairs, cycles)
    whole = packed // 128 * 128
    column = split + lax.broadcasted_iota(jnp.int32, (pairs, whole - split), 1)
    half = 4 * pairs

    @pl.loop(0, blocks, unroll=blocks <= 10)
    def _(i):
        part = pl.ds(pl.multiple_of(i * pairs, pairs), pairs)
        wide = jnp.broadcast_to(coeff_ref[pl.ds(i, 1)], (pairs, cycles, 8 * pairs))
        wide = jnp.where(mask, wide, 0.0).reshape(pairs * cycles, 8 * pairs)
        wide = wide.astype(jnp.bfloat16).astype(jnp.float32)
        lower = column < limit_ref[part]
        leg = leg_ref[part].reshape(pairs * cycles, packed)
        beyond = [
            jnp.sum(wide * leg[:, at : at + 1].astype(jnp.float32), axis=0, keepdims=True)
            for at in range(whole, packed)
        ]
        beyond.append(jnp.zeros((8 - len(beyond), 8 * pairs), jnp.float32))
        wide = jnp.concatenate([wide] + beyond, axis=0).T
        beyond = wide[half:, pairs * cycles : pairs * cycles + packed - whole].astype(jnp.bfloat16)
        wide = wide[:, : pairs * cycles].astype(jnp.bfloat16)
        left = jnp.dot(wide[:half], leg[:, :split], preferred_element_type=jnp.float32)
        right = jnp.dot(wide, leg[:, split:whole], preferred_element_type=jnp.float32)
        for s in range(2):
            for f in range(FIELDS):
                at = (s * FIELDS + f) * pairs
                out_vmem[s, f, 0, part, :split] = left[at : at + pairs].astype(jnp.bfloat16)
                low, high = right[at : at + pairs], right[half + at : half + at + pairs]
                out_vmem[s, f, 0, part, split:whole] = jnp.where(lower, low, high).astype(jnp.bfloat16)
                out_vmem[s, f, 0, part, whole:] = beyond[at : at + pairs]
        write(i).start()

    for i in range(blocks):
        write(i).wait()


def grid_kernel(
    points_dev, levs, split, length_hbm, weight_hbm, low_hbm, forcing_hbm, mixing_hbm, spec_hbm, leg_hbm,
    out_ref, limit_ref, leg_ref,
    length_ref, weight_ref, low_ref, forcing_ref, mixing_ref,
    cos_tab, sin_tab, cos_out, sin_out, grid_ref, force_ref,
    outgoing, incoming, partial, arrived, spec_vmem, four_ref, wave_ref,
    send_sem, recv_sem, send_back, recv_back, leg_sem, spec_sem, small_sem,
):
    blocks, cycles, wide = four_ref.shape
    pairs = wide // 8
    packed = leg_ref.shape[2]
    each = wide // 4

    def read_spec(i):
        part = pl.ds(pl.multiple_of(i * pairs, pairs), pairs)
        return pltpu.make_async_copy(
            spec_hbm.at[:, :, :, part], spec_vmem.at[:, :, :, part], spec_sem.at[i]
        )

    def read_leg(i):
        part = pl.ds(pl.multiple_of(i * pairs, pairs), pairs)
        return pltpu.make_async_copy(leg_hbm.at[part], leg_ref.at[part], leg_sem.at[i])

    small = [
        pltpu.make_async_copy(src, dst, small_sem.at[k])
        for k, (src, dst) in enumerate(
            (
                (low_hbm, low_ref), (length_hbm, length_ref), (weight_hbm, weight_ref),
                (forcing_hbm, forcing_ref), (mixing_hbm, mixing_ref),
            )
        )
    ]
    for copy in small[:3]:
        copy.start()

    rows = FIELDS * levs
    outer = cos_out.shape[0]
    used = pl.cdiv(points_dev, INNER)
    slots, _, lanes = incoming.shape
    bands = slots // levs
    band_id = lax.axis_index("band")
    lev_id = lax.axis_index("lev")
    me = band_id * levs + lev_id
    base = lev_id * points_dev
    barrier = pltpu.get_barrier_semaphore()

    def each_peer(act, midway=None):
        def of_band(flips, skip):
            band = toggled(band_id, flips, bands)
            for turn in range(levs - 1, skip - 1, -1):
                act(band, (lev_id + turn) % levs)

        if slots <= 64:
            for flips in range(bands - 1, 0, -1):
                of_band(flips, 0)
                if midway and flips == bands // 2:
                    midway()
        else:
            @pl.loop(1, bands)
            def _(step):
                of_band(bands - step, 0)

            if midway:
                midway()
        of_band(0, 1)

    def read_all():
        for i in range(blocks):
            read_spec(i).start()
            read_leg(i).start()
        for copy in small[3:]:
            copy.start()

    each_peer(
        lambda band, lev: pl.semaphore_signal(
            barrier, inc=1, device_id={"band": band, "lev": lev}, device_id_type=pl.DeviceIdType.MESH
        ),
        read_all,
    )

    for at, copy in enumerate(small[:3]):
        copy.wait()
    length = length_ref[band_id]
    inverse_length = 1.0 / jnp.full((1, lanes), length, jnp.int32).astype(jnp.float32)
    factor = inverse_length * weight_ref[band_id]

    own = blocks * pairs
    line = low_ref[...].reshape(1, bands * own)
    low = jnp.concatenate([line[:, k * own : (k + 1) * own] for k in range(bands)], axis=0)
    parts = [low, TRUNC - low]
    if lanes > blocks * each:
        parts.append(jnp.full((bands, lanes - blocks * each), 1 << 14, jnp.int32))
    wave_ref[...] = jnp.concatenate(parts, axis=1)
    mine = jnp.broadcast_to(wave_ref[pl.ds(band_id, 1), :].astype(jnp.float32), (8, lanes)).T
    limit_ref[...] = TRUNC + 1 - mine[: blocks * pairs, 0:1].astype(jnp.int32)

    twice, inverse_twice = 2 * length, 0.5 * inverse_length

    def tables(c):
        span = pl.ds(pl.multiple_of(c * lanes, lanes), lanes)
        wave = wave_ref[pl.ds(c, 1), :]
        eight = lax.broadcasted_iota(jnp.int32, (8, lanes), 0)
        c0, s0 = sincos(wave, eight * 2 + 1, twice, inverse_twice)
        c1, s1 = sincos(wave, eight * 16, twice, inverse_twice)
        c2, s2 = sincos(wave, eight * 128, twice, inverse_twice)
        steps = lax.broadcasted_iota(jnp.int32, (outer, lanes), 0)
        c3, s3 = sincos(wave, 2 * base + INNER - 1 + steps * (2 * INNER), twice, inverse_twice)
        cos_out[:, span] = c3
        sin_out[:, span] = s3
        for high in range(HALF // 64):
            ch, sh = c2[high : high + 1], s2[high : high + 1]
            cj, sj = ch * c1 - sh * s1, ch * s1 + sh * c1
            for mid in range(8):
                cm, sm = cj[mid : mid + 1], sj[mid : mid + 1]
                at = high * 64 + mid * 8
                cos_tab[at : at + 8, span] = (c0 * cm - s0 * sm).astype(jnp.bfloat16)
                sin_tab[at : at + 8, span] = (s0 * cm + c0 * sm).astype(jnp.bfloat16)

    mask = diagonal(pairs, cycles)
    column = split + lax.broadcasted_iota(jnp.int32, (pairs, packed - split), 1)
    inner = (((1,), (1,)), ((), ()))

    def legendre(i):
        part = pl.ds(pl.multiple_of(i * pairs, pairs), pairs)
        lower = column < limit_ref[part]
        whole, lows, highs = [], [], []
        for s in range(2):
            for f in range(FIELDS):
                whole.append(spec_vmem[s, f, 0, part, :split])
                row = spec_vmem[s, f, 0, part, split:].astype(jnp.float32)
                lows.append(jnp.where(lower, row, 0.0))
                highs.append(jnp.where(lower, 0.0, row))
        left = jnp.concatenate(whole, axis=0)
        right = jnp.concatenate(lows + highs, axis=0).astype(jnp.bfloat16)
        leg = leg_ref[part].reshape(pairs * cycles, packed)
        full = lax.dot_general(leg[:, split:], right, inner, preferred_element_type=jnp.float32)
        some = lax.dot_general(leg[:, :split], left, inner, preferred_element_type=jnp.float32)
        full = full + jnp.concatenate([some, jnp.zeros_like(some)], axis=1)
        full = full.reshape(pairs, cycles, 8 * pairs)
        four_ref[i] = jnp.sum(jnp.where(mask, full, 0.0), axis=0)

    def arrive(i):
        read_spec(i).wait()
        read_leg(i).wait()

    group = 2 if blocks % 2 == 0 else 1
    early = min(2, bands)

    pl.loop(0, early)(tables)

    @pl.loop(0, blocks // group)
    def _(step):
        first = step * group
        for at in range(group):
            arrive(first + at)
        for at in range(group):
            legendre(first + at)

    sides = []
    for k in range(4):
        parts = [
            four_ref[i, :, (4 * h + k) * pairs : (4 * h + k + 1) * pairs]
            for h in range(2)
            for i in range(blocks)
        ]
        if lanes > blocks * each:
            parts.append(jnp.zeros((cycles, lanes - blocks * each), jnp.float32))
        sides.append(jnp.concatenate(parts, axis=1))
    for j in range(cycles):
        block = jnp.concatenate([side[j : j + 1] for side in sides], axis=0)
        outgoing[j] = block.astype(jnp.bfloat16)

    pl.semaphore_wait(barrier, slots - 1)

    def send(source, target, here, there):
        def act(band, lev):
            pltpu.make_async_remote_copy(
                src_ref=source(band, lev), dst_ref=target.at[me], send_sem=here,
                recv_sem=there, device_id={"band": band, "lev": lev},
                device_id_type=pl.DeviceIdType.MESH,
            ).start()
        return act

    each_peer(send(lambda band, lev: outgoing.at[band], incoming, send_sem, recv_sem.at[band_id]))
    incoming[me] = outgoing[band_id]

    pl.loop(early, bands)(tables)

    def force_at(start):
        stop = min(start + HALF, points_dev)
        if stop <= start:
            return jnp.zeros((rows, HALF), jnp.float32)
        force = [forcing_ref[f, :, start:stop].astype(jnp.float32) for f in range(FIELDS)]
        force = jnp.concatenate(force, axis=0)
        if stop < start + HALF:
            rest = jnp.zeros((rows, start + HALF - stop), jnp.float32)
            force = jnp.concatenate([force, rest], axis=1)
        return force

    for copy in small[3:]:
        copy.wait()
    before = jnp.concatenate([force_at(a * INNER) for a in range(used)], axis=0)
    turned = lax.broadcasted_iota(jnp.int32, (HALF, HALF), 0) + lax.broadcasted_iota(
        jnp.int32, (HALF, HALF), 1
    )
    turned = jnp.where(turned == HALF - 1, 1.0, 0.0).astype(jnp.bfloat16)
    force_ref[0] = jnp.concatenate([force_at(a * INNER + HALF) for a in range(used)], axis=0)
    force_ref[1] = jnp.dot(before.astype(jnp.bfloat16), turned, preferred_element_type=jnp.float32)

    def wait_all(semaphore, buffer, count):
        most = buffer.at[pl.ds(0, count)]
        pltpu.make_async_copy(most, most, semaphore).wait()

    contract = (((1,), (1,)), ((), ()))
    near = 2 if bands % 2 == 0 else 1
    groups = bands // near

    def span_of(group):
        return pl.ds(pl.multiple_of(group * (near * lanes), near * lanes), near * lanes)

    def waves_of(group):
        return jnp.concatenate([wave_ref[pl.ds(group * near + at, 1), :] for at in range(near)], axis=1)

    def synthesis(group):
        span, wave = span_of(group), waves_of(group)
        gain = jnp.where(wave == 0, 1.0, 2.0)
        live = 2 * wave < length
        cells = [
            jnp.concatenate([incoming[(group * near + at) * levs + lev] for at in range(near)], axis=1)
            for lev in range(levs)
        ]
        cells = [cell.astype(jnp.float32) for cell in cells]
        order = [(f, lev) for f in range(FIELDS) for lev in range(levs)]
        re = jnp.concatenate([cells[lev][f : f + 1] for f, lev in order], axis=0)
        im = jnp.concatenate([cells[lev][FIELDS + f : FIELDS + f + 1] for f, lev in order], axis=0)
        re = jnp.where(live, re * gain, 0.0)
        im = jnp.where(live, im * -gain, 0.0)
        twist_re, twist_im = [], []
        for a in range(used):
            co, so = cos_out[a : a + 1, span], sin_out[a : a + 1, span]
            twist_re.append(re * co + im * so)
            twist_im.append(im * co - re * so)
        twist_re = jnp.concatenate(twist_re, axis=0).astype(jnp.bfloat16)
        twist_im = jnp.concatenate(twist_im, axis=0).astype(jnp.bfloat16)
        even = lax.dot_general(twist_re, cos_tab[:, span], contract, preferred_element_type=jnp.float32)
        odd = lax.dot_general(twist_im, sin_tab[:, span], contract, preferred_element_type=jnp.float32)
        return even, odd

    def wait_group(flips, own):
        group = toggled(band_id // near, flips, groups)
        for at in range(near):
            if own:
                first = (band_id + at) % near
                wait_all(recv_sem.at[group * near + first], incoming, levs - (at == 0))
            else:
                wait_all(recv_sem.at[group * near + at], incoming, levs)
        return group

    if groups <= 8:
        even, odd = 0.0, 0.0
        for last in range(groups - 1, -1, -STEP):
            these = range(last, max(last - STEP, -1), -1)
            these = [wait_group(flips, flips == 0) for flips in these]
            for group in these:
                half = synthesis(group)
                even, odd = even + half[0], odd + half[1]
    else:
        grid_ref[0], grid_ref[1] = synthesis(wait_group(0, True))

        @pl.loop(1, groups)
        def _(flips):
            half = synthesis(wait_group(flips, False))
            grid_ref[0] += half[0]
            grid_ref[1] += half[1]

        even, odd = grid_ref[0], grid_ref[1]

    lane = lax.broadcasted_iota(jnp.int32, (rows, HALF), 1)
    mixing = jnp.concatenate([mixing_ref[f].astype(jnp.float32) for f in range(FIELDS)], axis=0)

    def physics(side, values, a):
        point = a * INNER + (HALF - 1 - lane if side else HALF + lane)
        inside = (point < points_dev) & (base + point < length)
        cell = jnp.where(inside, values, 0.0)
        product = (cell[:levs] * cell[levs:]).astype(jnp.bfloat16).astype(jnp.float32)
        total = cell + force_ref[side, a * rows : (a + 1) * rows]
        for l2 in range(levs):
            total = total + mixing[:, l2 : l2 + 1] * product[l2 : l2 + 1]
        return jnp.where(inside, total, 0.0)

    sums, gaps = [], []
    for a in range(used):
        at = slice(a * rows, (a + 1) * rows)
        after, before = physics(0, even[at] + odd[at], a), physics(1, even[at] - odd[at], a)
        sums.append(after + before)
        gaps.append(after - before)
    sums = jnp.concatenate(sums, axis=0).astype(jnp.bfloat16)
    gaps = jnp.concatenate(gaps, axis=0).astype(jnp.bfloat16)

    send_partial = send(
        lambda band, lev: partial.at[band * levs + lev], arrived, send_back, recv_back
    )

    def analysis(band):
        pieces = []
        for start in range(0, lanes, CHUNK):
            size = min(CHUNK, lanes - start)
            span = pl.ds(pl.multiple_of(band * lanes + start, 128), size)
            cos_part = jnp.dot(sums, cos_tab[:, span], preferred_element_type=jnp.float32)
            sin_part = jnp.dot(gaps, sin_tab[:, span], preferred_element_type=jnp.float32)
            re = jnp.zeros((rows, size), jnp.float32)
            im = jnp.zeros((rows, size), jnp.float32)
            for a in range(used):
                co, so = cos_out[a : a + 1, span], sin_out[a : a + 1, span]
                cp, sp = cos_part[a * rows : (a + 1) * rows], sin_part[a * rows : (a + 1) * rows]
                re = re + (cp * co - sp * so)
                im = im + (cp * so + sp * co)
            pieces.append((re, im))
        re, im = (jnp.concatenate(side, axis=1) for side in zip(*pieces))
        keep = 2 * wave_ref[pl.ds(band, 1), :] < length
        re = jnp.where(keep, re * factor, 0.0)
        im = jnp.where(keep, im * -factor, 0.0)
        for lev in range(levs):
            picks = [side[f * levs + lev : f * levs + lev + 1] for side in (re, im) for f in range(FIELDS)]
            partial[band * levs + lev] = jnp.concatenate(picks, axis=0).astype(jnp.bfloat16)

    def serve(band):
        analysis(band)
        for turn in range(levs - 1, 0, -1):
            send_partial(band, (lev_id + turn) % levs)
        pl.when(band != band_id)(functools.partial(send_partial, band, lev_id))

    if bands <= 8:
        for band in range(bands):
            serve(band)
    else:
        pl.loop(0, bands)(serve)
    arrived[me] = partial[me]

    wait_all(recv_back, arrived, slots - 1)
    levels_sum = []
    for j in range(cycles):
        total = arrived[j * levs].astype(jnp.float32)
        for lev in range(1, levs):
            total = total + arrived[j * levs + lev].astype(jnp.float32)
        levels_sum.append(total)
    for k in range(4):
        side = jnp.concatenate([total[k : k + 1] for total in levels_sum], axis=0)
        for h in range(2):
            for i in range(blocks):
                at, lane = (4 * h + k) * pairs, (h * blocks + i) * pairs
                out_ref[i, :, at : at + pairs] = side[:, lane : lane + pairs]
    wait_all(send_sem, incoming, slots - 1)
    wait_all(send_back, arrived, slots - 1)


def on_device(spectral, legendre, cycle_len, pair_wave, quad_weight, forcing, mixing):
    band_count = lax.axis_size("band")
    lev_count = lax.axis_size("lev")
    pair_dev = spectral.shape[3]
    cycles = legendre.shape[1]
    levels, points_dev = forcing.shape[1], forcing.shape[3]
    rows = FIELDS * levels
    pairs = pair_block(pair_dev)
    blocks = pair_dev // pairs

    each_band = pl.cdiv(2 * pair_dev, 128) * 128
    waves = band_count * each_band
    used = pl.cdiv(points_dev, INNER)
    outer = pl.cdiv(used, 8) * 8
    force = forcing.reshape(FIELDS, levels, points_dev)
    vmem = pl.BlockSpec(memory_space=pltpu.VMEM)
    slots = band_count * lev_count
    message = pltpu.VMEM((slots, 2 * FIELDS, each_band), jnp.bfloat16)
    split = (TRUNC + 2 - pair_wave.shape[0]) // 128 * 128
    hbm = pl.BlockSpec(memory_space=pltpu.HBM)
    coeff, limit, leg = pl.pallas_call(
        functools.partial(grid_kernel, points_dev, lev_count, split),
        in_specs=[hbm] * 7,
        out_specs=[vmem] * 3,
        out_shape=[
            pltpu.VMEM((blocks, cycles, 8 * pairs), jnp.float32),
            pltpu.VMEM((pair_dev, 1), jnp.int32),
            pltpu.VMEM(legendre.shape, jnp.bfloat16),
        ],
        scratch_shapes=[
            pltpu.SMEM(cycle_len.shape, jnp.int32),
            pltpu.SMEM(quad_weight.shape, jnp.float32),
            pltpu.VMEM(pair_wave.shape, jnp.int32),
            pltpu.VMEM(force.shape, jnp.bfloat16),
            pltpu.VMEM(mixing.shape, jnp.bfloat16),
            pltpu.VMEM((HALF, waves), jnp.bfloat16),
            pltpu.VMEM((HALF, waves), jnp.bfloat16),
            pltpu.VMEM((outer, waves), jnp.float32),
            pltpu.VMEM((outer, waves), jnp.float32),
            pltpu.VMEM((2, used * rows, HALF), jnp.float32),
            pltpu.VMEM((2, used * rows, HALF), jnp.float32),
            pltpu.VMEM((cycles, 2 * FIELDS, each_band), jnp.bfloat16),
            message, message, message,
            pltpu.VMEM(spectral.shape, jnp.bfloat16),
            pltpu.VMEM((blocks, cycles, 8 * pairs), jnp.float32),
            pltpu.VMEM((band_count, each_band), jnp.int32),
            pltpu.SemaphoreType.DMA,
            pltpu.SemaphoreType.DMA((band_count,)),
            pltpu.SemaphoreType.DMA,
            pltpu.SemaphoreType.DMA,
            pltpu.SemaphoreType.DMA((blocks,)),
            pltpu.SemaphoreType.DMA((blocks,)),
            pltpu.SemaphoreType.DMA((5,)),
        ],
        compiler_params=pltpu.CompilerParams(
            collective_id=0, has_side_effects=True, vmem_limit_bytes=VMEM_LIMIT
        ),
    )(
        *(
            pltpu.with_memory_space_constraint(array, pltpu.HBM)
            for array in (cycle_len, quad_weight, pair_wave, force, mixing, spectral, legendre)
        )
    )
    return pl.pallas_call(
        functools.partial(direct_kernel, split),
        in_specs=[vmem, vmem, vmem],
        out_specs=hbm,
        out_shape=jax.ShapeDtypeStruct(spectral.shape, jnp.bfloat16),
        scratch_shapes=[pltpu.VMEM(spectral.shape, jnp.bfloat16), pltpu.SemaphoreType.DMA((blocks,))],
        compiler_params=pltpu.CompilerParams(vmem_limit_bytes=VMEM_LIMIT),
    )(limit, coeff, leg)


def solution(mesh):
    return jax.shard_map(
        on_device,
        mesh=mesh,
        in_specs=(
            P(None, None, "lev", "band", None),
            P("band", None, None),
            P(),
            P(),
            P(),
            P(None, None, "band", "lev"),
            P(),
        ),
        out_specs=P(None, None, "lev", "band", None),
        check_vma=False,
    )
```

```python
import functools

import jax
import jax.numpy as jnp
from jax import lax
from jax.experimental import pallas as pl
from jax.experimental.pallas import tpu as pltpu
from jax.sharding import PartitionSpec as P

TRUNC = 2559
FIELDS = 2
HALF = 128
INNER = 2 * HALF
VMEM_LIMIT = 32 << 20
STEP = 2
CHUNK = 256
TWO_PI = 6.283185307179586


def pair_block(pair_dev):
    return 16 if pair_dev % 16 == 0 else 8


def sincos(wave, point, length, inverse_length):
    number = wave * point
    turns = jnp.floor(number.astype(jnp.float32) * inverse_length).astype(jnp.int32)
    residue = (number - turns * length).astype(jnp.float32) * inverse_length
    quarter = jnp.floor(residue * 4.0 + 0.5)
    t = (residue - quarter * 0.25) * TWO_PI
    t2 = t * t
    sin_t = t * (1.0 + t2 * (-1.0 / 6 + t2 * (1.0 / 120 + t2 * (-1.0 / 5040 + t2 * (1.0 / 362880)))))
    cos_t = 1.0 + t2 * (
        -0.5 + t2 * (1.0 / 24 + t2 * (-1.0 / 720 + t2 * (1.0 / 40320 + t2 * (-1.0 / 3628800))))
    )
    q = quarter.astype(jnp.int32)
    swap = (q & 1) == 1
    cos_v = jnp.where(swap, sin_t, cos_t)
    sin_v = jnp.where(swap, cos_t, sin_t)
    cos_v = jnp.where(((q + 1) & 2) == 2, -cos_v, cos_v)
    sin_v = jnp.where((q & 2) == 2, -sin_v, sin_v)
    return cos_v, sin_v


def diagonal(pairs, cycles):
    rows = lax.broadcasted_iota(jnp.int32, (pairs, cycles, 8 * pairs), 0)
    lanes = lax.broadcasted_iota(jnp.int32, (pairs, cycles, 8 * pairs), 2) % pairs
    return rows == lanes


def toggled(index, flips, count):
    if count & (count - 1):
        return (index + flips) % count
    result, bit = 0, 1
    while bit < count:
        result = result + (index // bit + flips // bit) % 2 * bit
        bit *= 2
    return result


def direct_kernel(split, limit_ref, coeff_ref, leg_ref, out_hbm, out_vmem, out_sem):
    blocks, cycles, wide_lanes = coeff_ref.shape
    pairs = wide_lanes // 8
    packed = leg_ref.shape[2]

    def write(i):
        part = pl.ds(pl.multiple_of(i * pairs, pairs), pairs)
        return pltpu.make_async_copy(
            out_vmem.at[:, :, :, part], out_hbm.at[:, :, :, part], out_sem.at[i]
        )

    mask = diagonal(pairs, cycles)
    whole = packed // 128 * 128
    column = split + lax.broadcasted_iota(jnp.int32, (pairs, whole - split), 1)
    half = 4 * pairs

    @pl.loop(0, blocks, unroll=blocks <= 10)
    def _(i):
        part = pl.ds(pl.multiple_of(i * pairs, pairs), pairs)
        wide = jnp.broadcast_to(coeff_ref[pl.ds(i, 1)], (pairs, cycles, 8 * pairs))
        wide = jnp.where(mask, wide, 0.0).reshape(pairs * cycles, 8 * pairs)
        wide = wide.astype(jnp.bfloat16).astype(jnp.float32)
        lower = column < limit_ref[part]
        leg = leg_ref[part].reshape(pairs * cycles, packed)
        beyond = [
            jnp.sum(wide * leg[:, at : at + 1].astype(jnp.float32), axis=0, keepdims=True)
            for at in range(whole, packed)
        ]
        beyond.append(jnp.zeros((8 - len(beyond), 8 * pairs), jnp.float32))
        wide = jnp.concatenate([wide] + beyond, axis=0).T
        beyond = wide[half:, pairs * cycles : pairs * cycles + packed - whole].astype(jnp.bfloat16)
        wide = wide[:, : pairs * cycles].astype(jnp.bfloat16)
        left = jnp.dot(wide[:half], leg[:, :split], preferred_element_type=jnp.float32)
        right = jnp.dot(wide, leg[:, split:whole], preferred_element_type=jnp.float32)
        for s in range(2):
            for f in range(FIELDS):
                at = (s * FIELDS + f) * pairs
                out_vmem[s, f, 0, part, :split] = left[at : at + pairs].astype(jnp.bfloat16)
                low, high = right[at : at + pairs], right[half + at : half + at + pairs]
                out_vmem[s, f, 0, part, split:whole] = jnp.where(lower, low, high).astype(jnp.bfloat16)
                out_vmem[s, f, 0, part, whole:] = beyond[at : at + pairs]
        write(i).start()

    for i in range(blocks):
        write(i).wait()


def grid_kernel(
    points_dev, levs, split, length_hbm, weight_hbm, low_hbm, forcing_hbm, mixing_hbm, spec_hbm, leg_hbm,
    out_ref, limit_ref, leg_ref,
    length_ref, weight_ref, low_ref, forcing_ref, mixing_ref,
    cos_tab, sin_tab, cos_out, sin_out, grid_ref, force_ref,
    outgoing, incoming, partial, arrived, spec_vmem, four_ref, wave_ref,
    send_sem, recv_sem, send_back, recv_back, leg_sem, spec_sem, small_sem,
):
    blocks, cycles, wide = four_ref.shape
    pairs = wide // 8
    packed = leg_ref.shape[2]
    each = wide // 4

    def read_spec(i):
        part = pl.ds(pl.multiple_of(i * pairs, pairs), pairs)
        return pltpu.make_async_copy(
            spec_hbm.at[:, :, :, part], spec_vmem.at[:, :, :, part], spec_sem.at[i]
        )

    def read_leg(i):
        part = pl.ds(pl.multiple_of(i * pairs, pairs), pairs)
        return pltpu.make_async_copy(leg_hbm.at[part], leg_ref.at[part], leg_sem.at[i])

    small = [
        pltpu.make_async_copy(src, dst, small_sem.at[k])
        for k, (src, dst) in enumerate(
            (
                (low_hbm, low_ref), (length_hbm, length_ref), (weight_hbm, weight_ref),
                (forcing_hbm, forcing_ref), (mixing_hbm, mixing_ref),
            )
        )
    ]
    for copy in small[:3]:
        copy.start()

    rows = FIELDS * levs
    outer = cos_out.shape[0]
    used = pl.cdiv(points_dev, INNER)
    slots, _, lanes = incoming.shape
    bands = slots // levs
    band_id = lax.axis_index("band")
    lev_id = lax.axis_index("lev")
    me = band_id * levs + lev_id
    base = lev_id * points_dev
    barrier = pltpu.get_barrier_semaphore()

    def each_peer(act, midway=None):
        def of_band(flips, skip):
            band = toggled(band_id, flips, bands)
            for turn in range(levs - 1, skip - 1, -1):
                act(band, (lev_id + turn) % levs)

        if slots <= 64:
            for flips in range(bands - 1, 0, -1):
                of_band(flips, 0)
                if midway and flips == bands // 2:
                    midway()
        else:
            @pl.loop(1, bands)
            def _(step):
                of_band(bands - step, 0)

            if midway:
                midway()
        of_band(0, 1)

    def read_all():
        for i in range(blocks):
            read_spec(i).start()
            read_leg(i).start()
        for copy in small[3:]:
            copy.start()

    each_peer(
        lambda band, lev: pl.semaphore_signal(
            barrier, inc=1, device_id={"band": band, "lev": lev}, device_id_type=pl.DeviceIdType.MESH
        ),
        read_all,
    )

    for at, copy in enumerate(small[:3]):
        copy.wait()
    length = length_ref[band_id]
    inverse_length = 1.0 / jnp.full((1, lanes), length, jnp.int32).astype(jnp.float32)
    factor = inverse_length * weight_ref[band_id]

    own = blocks * pairs
    line = low_ref[...].reshape(1, bands * own)
    low = jnp.concatenate([line[:, k * own : (k + 1) * own] for k in range(bands)], axis=0)
    parts = [low, TRUNC - low]
    if lanes > blocks * each:
        parts.append(jnp.full((bands, lanes - blocks * each), 1 << 14, jnp.int32))
    wave_ref[...] = jnp.concatenate(parts, axis=1)
    mine = jnp.broadcast_to(wave_ref[pl.ds(band_id, 1), :].astype(jnp.float32), (8, lanes)).T
    limit_ref[...] = TRUNC + 1 - mine[: blocks * pairs, 0:1].astype(jnp.int32)

    twice, inverse_twice = 2 * length, 0.5 * inverse_length

    def tables(c):
        span = pl.ds(pl.multiple_of(c * lanes, lanes), lanes)
        wave = wave_ref[pl.ds(c, 1), :]
        eight = lax.broadcasted_iota(jnp.int32, (8, lanes), 0)
        c0, s0 = sincos(wave, eight * 2 + 1, twice, inverse_twice)
        c1, s1 = sincos(wave, eight * 16, twice, inverse_twice)
        c2, s2 = sincos(wave, eight * 128, twice, inverse_twice)
        steps = lax.broadcasted_iota(jnp.int32, (outer, lanes), 0)
        c3, s3 = sincos(wave, 2 * base + INNER - 1 + steps * (2 * INNER), twice, inverse_twice)
        cos_out[:, span] = c3
        sin_out[:, span] = s3
        for high in range(HALF // 64):
            ch, sh = c2[high : high + 1], s2[high : high + 1]
            cj, sj = ch * c1 - sh * s1, ch * s1 + sh * c1
            for mid in range(8):
                cm, sm = cj[mid : mid + 1], sj[mid : mid + 1]
                at = high * 64 + mid * 8
                cos_tab[at : at + 8, span] = (c0 * cm - s0 * sm).astype(jnp.bfloat16)
                sin_tab[at : at + 8, span] = (s0 * cm + c0 * sm).astype(jnp.bfloat16)

    mask = diagonal(pairs, cycles)
    column = split + lax.broadcasted_iota(jnp.int32, (pairs, packed - split), 1)
    inner = (((1,), (1,)), ((), ()))

    def legendre(i):
        part = pl.ds(pl.multiple_of(i * pairs, pairs), pairs)
        lower = column < limit_ref[part]
        whole, lows, highs = [], [], []
        for s in range(2):
            for f in range(FIELDS):
                whole.append(spec_vmem[s, f, 0, part, :split])
                row = spec_vmem[s, f, 0, part, split:].astype(jnp.float32)
                lows.append(jnp.where(lower, row, 0.0))
                highs.append(jnp.where(lower, 0.0, row))
        left = jnp.concatenate(whole, axis=0)
        right = jnp.concatenate(lows + highs, axis=0).astype(jnp.bfloat16)
        leg = leg_ref[part].reshape(pairs * cycles, packed)
        full = lax.dot_general(leg[:, split:], right, inner, preferred_element_type=jnp.float32)
        some = lax.dot_general(leg[:, :split], left, inner, preferred_element_type=jnp.float32)
        full = full + jnp.concatenate([some, jnp.zeros_like(some)], axis=1)
        full = full.reshape(pairs, cycles, 8 * pairs)
        four_ref[i] = jnp.sum(jnp.where(mask, full, 0.0), axis=0)

    def arrive(i):
        read_spec(i).wait()
        read_leg(i).wait()

    group = 2 if blocks % 2 == 0 else 1
    early = min(2, bands)

    pl.loop(0, early)(tables)

    @pl.loop(0, blocks // group)
    def _(step):
        first = step * group
        for at in range(group):
            arrive(first + at)
        for at in range(group):
            legendre(first + at)

    sides = []
    for k in range(4):
        parts = [
            four_ref[i, :, (4 * h + k) * pairs : (4 * h + k + 1) * pairs]
            for h in range(2)
            for i in range(blocks)
        ]
        if lanes > blocks * each:
            parts.append(jnp.zeros((cycles, lanes - blocks * each), jnp.float32))
        sides.append(jnp.concatenate(parts, axis=1))
    for j in range(cycles):
        block = jnp.concatenate([side[j : j + 1] for side in sides], axis=0)
        outgoing[j] = block.astype(jnp.bfloat16)

    pl.semaphore_wait(barrier, slots - 1)

    def send(source, target, here, there):
        def act(band, lev):
            pltpu.make_async_remote_copy(
                src_ref=source(band, lev), dst_ref=target.at[me], send_sem=here,
                recv_sem=there, device_id={"band": band, "lev": lev},
                device_id_type=pl.DeviceIdType.MESH,
            ).start()
        return act

    each_peer(send(lambda band, lev: outgoing.at[band], incoming, send_sem, recv_sem.at[band_id]))
    incoming[me] = outgoing[band_id]

    pl.loop(early, bands)(tables)

    def force_at(start):
        stop = min(start + HALF, points_dev)
        if stop <= start:
            return jnp.zeros((rows, HALF), jnp.float32)
        force = [forcing_ref[f, :, start:stop].astype(jnp.float32) for f in range(FIELDS)]
        force = jnp.concatenate(force, axis=0)
        if stop < start + HALF:
            rest = jnp.zeros((rows, start + HALF - stop), jnp.float32)
            force = jnp.concatenate([force, rest], axis=1)
        return force

    for copy in small[3:]:
        copy.wait()
    before = jnp.concatenate([force_at(a * INNER) for a in range(used)], axis=0)
    turned = lax.broadcasted_iota(jnp.int32, (HALF, HALF), 0) + lax.broadcasted_iota(
        jnp.int32, (HALF, HALF), 1
    )
    turned = jnp.where(turned == HALF - 1, 1.0, 0.0).astype(jnp.bfloat16)
    force_ref[0] = jnp.concatenate([force_at(a * INNER + HALF) for a in range(used)], axis=0)
    force_ref[1] = jnp.dot(before.astype(jnp.bfloat16), turned, preferred_element_type=jnp.float32)

    def wait_all(semaphore, buffer, count):
        most = buffer.at[pl.ds(0, count)]
        pltpu.make_async_copy(most, most, semaphore).wait()

    contract = (((1,), (1,)), ((), ()))
    near = 2 if bands % 2 == 0 else 1
    groups = bands // near

    def span_of(group):
        return pl.ds(pl.multiple_of(group * (near * lanes), near * lanes), near * lanes)

    def waves_of(group):
        return jnp.concatenate([wave_ref[pl.ds(group * near + at, 1), :] for at in range(near)], axis=1)

    def synthesis(group):
        span, wave = span_of(group), waves_of(group)
        gain = jnp.where(wave == 0, 1.0, 2.0)
        live = 2 * wave < length
        cells = [
            jnp.concatenate([incoming[(group * near + at) * levs + lev] for at in range(near)], axis=1)
            for lev in range(levs)
        ]
        cells = [cell.astype(jnp.float32) for cell in cells]
        order = [(f, lev) for f in range(FIELDS) for lev in range(levs)]
        re = jnp.concatenate([cells[lev][f : f + 1] for f, lev in order], axis=0)
        im = jnp.concatenate([cells[lev][FIELDS + f : FIELDS + f + 1] for f, lev in order], axis=0)
        re = jnp.where(live, re * gain, 0.0)
        im = jnp.where(live, im * -gain, 0.0)
        twist_re, twist_im = [], []
        for a in range(used):
            co, so = cos_out[a : a + 1, span], sin_out[a : a + 1, span]
            twist_re.append(re * co + im * so)
            twist_im.append(im * co - re * so)
        twist_re = jnp.concatenate(twist_re, axis=0).astype(jnp.bfloat16)
        twist_im = jnp.concatenate(twist_im, axis=0).astype(jnp.bfloat16)
        even = lax.dot_general(twist_re, cos_tab[:, span], contract, preferred_element_type=jnp.float32)
        odd = lax.dot_general(twist_im, sin_tab[:, span], contract, preferred_element_type=jnp.float32)
        return even, odd

    def wait_group(flips, own):
        group = toggled(band_id // near, flips, groups)
        for at in range(near):
            if own:
                first = (band_id + at) % near
                wait_all(recv_sem.at[group * near + first], incoming, levs - (at == 0))
            else:
                wait_all(recv_sem.at[group * near + at], incoming, levs)
        return group

    if groups <= 8:
        even, odd = 0.0, 0.0
        for last in range(groups - 1, -1, -STEP):
            these = range(last, max(last - STEP, -1), -1)
            these = [wait_group(flips, flips == 0) for flips in these]
            for group in these:
                half = synthesis(group)
                even, odd = even + half[0], odd + half[1]
    else:
        grid_ref[0], grid_ref[1] = synthesis(wait_group(0, True))

        @pl.loop(1, groups)
        def _(flips):
            half = synthesis(wait_group(flips, False))
            grid_ref[0] += half[0]
            grid_ref[1] += half[1]

        even, odd = grid_ref[0], grid_ref[1]

    lane = lax.broadcasted_iota(jnp.int32, (rows, HALF), 1)
    mixing = jnp.concatenate([mixing_ref[f].astype(jnp.float32) for f in range(FIELDS)], axis=0)

    def physics(side, values, a):
        point = a * INNER + (HALF - 1 - lane if side else HALF + lane)
        inside = (point < points_dev) & (base + point < length)
        cell = jnp.where(inside, values, 0.0)
        product = (cell[:levs] * cell[levs:]).astype(jnp.bfloat16).astype(jnp.float32)
        total = cell + force_ref[side, a * rows : (a + 1) * rows]
        for l2 in range(levs):
            total = total + mixing[:, l2 : l2 + 1] * product[l2 : l2 + 1]
        return jnp.where(inside, total, 0.0)

    sums, gaps = [], []
    for a in range(used):
        at = slice(a * rows, (a + 1) * rows)
        after, before = physics(0, even[at] + odd[at], a), physics(1, even[at] - odd[at], a)
        sums.append(after + before)
        gaps.append(after - before)
    sums = jnp.concatenate(sums, axis=0).astype(jnp.bfloat16)
    gaps = jnp.concatenate(gaps, axis=0).astype(jnp.bfloat16)

    send_partial = send(
        lambda band, lev: partial.at[band * levs + lev], arrived, send_back, recv_back
    )

    def analysis(band):
        pieces = []
        for start in range(0, lanes, CHUNK):
            size = min(CHUNK, lanes - start)
            span = pl.ds(pl.multiple_of(band * lanes + start, 128), size)
            cos_part = jnp.dot(sums, cos_tab[:, span], preferred_element_type=jnp.float32)
            sin_part = jnp.dot(gaps, sin_tab[:, span], preferred_element_type=jnp.float32)
            re = jnp.zeros((rows, size), jnp.float32)
            im = jnp.zeros((rows, size), jnp.float32)
            for a in range(used):
                co, so = cos_out[a : a + 1, span], sin_out[a : a + 1, span]
                cp, sp = cos_part[a * rows : (a + 1) * rows], sin_part[a * rows : (a + 1) * rows]
                re = re + (cp * co - sp * so)
                im = im + (cp * so + sp * co)
            pieces.append((re, im))
        re, im = (jnp.concatenate(side, axis=1) for side in zip(*pieces))
        keep = 2 * wave_ref[pl.ds(band, 1), :] < length
        re = jnp.where(keep, re * factor, 0.0)
        im = jnp.where(keep, im * -factor, 0.0)
        for lev in range(levs):
            picks = [side[f * levs + lev : f * levs + lev + 1] for side in (re, im) for f in range(FIELDS)]
            partial[band * levs + lev] = jnp.concatenate(picks, axis=0).astype(jnp.bfloat16)

    def serve(band):
        analysis(band)
        for lev in range(levs):
            pl.when((band != band_id) | (lev != lev_id))(functools.partial(send_partial, band, lev))

    if bands <= 8:
        for band in range(bands):
            serve(band)
    else:
        pl.loop(0, bands)(serve)
    arrived[me] = partial[me]

    wait_all(recv_back, arrived, slots - 1)
    levels_sum = []
    for j in range(cycles):
        total = arrived[j * levs].astype(jnp.float32)
        for lev in range(1, levs):
            total = total + arrived[j * levs + lev].astype(jnp.float32)
        levels_sum.append(total)
    for k in range(4):
        side = jnp.concatenate([total[k : k + 1] for total in levels_sum], axis=0)
        for h in range(2):
            for i in range(blocks):
                at, lane = (4 * h + k) * pairs, (h * blocks + i) * pairs
                out_ref[i, :, at : at + pairs] = side[:, lane : lane + pairs]
    wait_all(send_sem, incoming, slots - 1)
    wait_all(send_back, arrived, slots - 1)


def on_device(spectral, legendre, cycle_len, pair_wave, quad_weight, forcing, mixing):
    band_count = lax.axis_size("band")
    lev_count = lax.axis_size("lev")
    pair_dev = spectral.shape[3]
    cycles = legendre.shape[1]
    levels, points_dev = forcing.shape[1], forcing.shape[3]
    rows = FIELDS * levels
    pairs = pair_block(pair_dev)
    blocks = pair_dev // pairs

    each_band = pl.cdiv(2 * pair_dev, 128) * 128
    waves = band_count * each_band
    used = pl.cdiv(points_dev, INNER)
    outer = pl.cdiv(used, 8) * 8
    force = forcing.reshape(FIELDS, levels, points_dev)
    vmem = pl.BlockSpec(memory_space=pltpu.VMEM)
    slots = band_count * lev_count
    message = pltpu.VMEM((slots, 2 * FIELDS, each_band), jnp.bfloat16)
    split = (TRUNC + 2 - pair_wave.shape[0]) // 128 * 128
    hbm = pl.BlockSpec(memory_space=pltpu.HBM)
    coeff, limit, leg = pl.pallas_call(
        functools.partial(grid_kernel, points_dev, lev_count, split),
        in_specs=[hbm] * 7,
        out_specs=[vmem] * 3,
        out_shape=[
            pltpu.VMEM((blocks, cycles, 8 * pairs), jnp.float32),
            pltpu.VMEM((pair_dev, 1), jnp.int32),
            pltpu.VMEM(legendre.shape, jnp.bfloat16),
        ],
        scratch_shapes=[
            pltpu.SMEM(cycle_len.shape, jnp.int32),
            pltpu.SMEM(quad_weight.shape, jnp.float32),
            pltpu.VMEM(pair_wave.shape, jnp.int32),
            pltpu.VMEM(force.shape, jnp.bfloat16),
            pltpu.VMEM(mixing.shape, jnp.bfloat16),
            pltpu.VMEM((HALF, waves), jnp.bfloat16),
            pltpu.VMEM((HALF, waves), jnp.bfloat16),
            pltpu.VMEM((outer, waves), jnp.float32),
            pltpu.VMEM((outer, waves), jnp.float32),
            pltpu.VMEM((2, used * rows, HALF), jnp.float32),
            pltpu.VMEM((2, used * rows, HALF), jnp.float32),
            pltpu.VMEM((cycles, 2 * FIELDS, each_band), jnp.bfloat16),
            message, message, message,
            pltpu.VMEM(spectral.shape, jnp.bfloat16),
            pltpu.VMEM((blocks, cycles, 8 * pairs), jnp.float32),
            pltpu.VMEM((band_count, each_band), jnp.int32),
            pltpu.SemaphoreType.DMA,
            pltpu.SemaphoreType.DMA((band_count,)),
            pltpu.SemaphoreType.DMA,
            pltpu.SemaphoreType.DMA,
            pltpu.SemaphoreType.DMA((blocks,)),
            pltpu.SemaphoreType.DMA((blocks,)),
            pltpu.SemaphoreType.DMA((5,)),
        ],
        compiler_params=pltpu.CompilerParams(
            collective_id=0, has_side_effects=True, vmem_limit_bytes=VMEM_LIMIT
        ),
    )(
        *(
            pltpu.with_memory_space_constraint(array, pltpu.HBM)
            for array in (cycle_len, quad_weight, pair_wave, force, mixing, spectral, legendre)
        )
    )
    return pl.pallas_call(
        functools.partial(direct_kernel, split),
        in_specs=[vmem, vmem, vmem],
        out_specs=hbm,
        out_shape=jax.ShapeDtypeStruct(spectral.shape, jnp.bfloat16),
        scratch_shapes=[pltpu.VMEM(spectral.shape, jnp.bfloat16), pltpu.SemaphoreType.DMA((blocks,))],
        compiler_params=pltpu.CompilerParams(vmem_limit_bytes=VMEM_LIMIT),
    )(limit, coeff, leg)


def solution(mesh):
    return jax.shard_map(
        on_device,
        mesh=mesh,
        in_specs=(
            P(None, None, "lev", "band", None),
            P("band", None, None),
            P(),
            P(),
            P(),
            P(None, None, "band", "lev"),
            P(),
        ),
        out_specs=P(None, None, "lev", "band", None),
        check_vma=False,
    )
```

```python
import functools

import jax
import jax.numpy as jnp
from jax import lax
from jax.experimental import pallas as pl
from jax.experimental.pallas import tpu as pltpu
from jax.sharding import PartitionSpec as P

TRUNC = 2559
FIELDS = 2
HALF = 128
INNER = 2 * HALF
VMEM_LIMIT = 32 << 20
STEP = 2
CHUNK = 256
TWO_PI = 6.283185307179586


def pair_block(pair_dev):
    return 16 if pair_dev % 16 == 0 else 8


def sincos(wave, point, length, inverse_length):
    number = wave * point
    turns = jnp.floor(number.astype(jnp.float32) * inverse_length).astype(jnp.int32)
    residue = (number - turns * length).astype(jnp.float32) * inverse_length
    quarter = jnp.floor(residue * 4.0 + 0.5)
    t = (residue - quarter * 0.25) * TWO_PI
    t2 = t * t
    sin_t = t * (1.0 + t2 * (-1.0 / 6 + t2 * (1.0 / 120 + t2 * (-1.0 / 5040 + t2 * (1.0 / 362880)))))
    cos_t = 1.0 + t2 * (
        -0.5 + t2 * (1.0 / 24 + t2 * (-1.0 / 720 + t2 * (1.0 / 40320 + t2 * (-1.0 / 3628800))))
    )
    q = quarter.astype(jnp.int32)
    swap = (q & 1) == 1
    cos_v = jnp.where(swap, sin_t, cos_t)
    sin_v = jnp.where(swap, cos_t, sin_t)
    cos_v = jnp.where(((q + 1) & 2) == 2, -cos_v, cos_v)
    sin_v = jnp.where((q & 2) == 2, -sin_v, sin_v)
    return cos_v, sin_v


def diagonal(pairs, cycles):
    rows = lax.broadcasted_iota(jnp.int32, (pairs, cycles, 8 * pairs), 0)
    lanes = lax.broadcasted_iota(jnp.int32, (pairs, cycles, 8 * pairs), 2) % pairs
    return rows == lanes


def toggled(index, flips, count):
    if count & (count - 1):
        return (index + flips) % count
    result, bit = 0, 1
    while bit < count:
        result = result + (index // bit + flips // bit) % 2 * bit
        bit *= 2
    return result


def direct_kernel(split, limit_ref, coeff_ref, leg_ref, out_hbm, out_vmem, out_sem):
    blocks, cycles, wide_lanes = coeff_ref.shape
    pairs = wide_lanes // 8
    packed = leg_ref.shape[2]

    def write(i):
        part = pl.ds(pl.multiple_of(i * pairs, pairs), pairs)
        return pltpu.make_async_copy(
            out_vmem.at[:, :, :, part], out_hbm.at[:, :, :, part], out_sem.at[i]
        )

    mask = diagonal(pairs, cycles)
    whole = packed // 128 * 128
    column = split + lax.broadcasted_iota(jnp.int32, (pairs, whole - split), 1)
    half = 4 * pairs

    @pl.loop(0, blocks, unroll=blocks <= 10)
    def _(i):
        part = pl.ds(pl.multiple_of(i * pairs, pairs), pairs)
        wide = jnp.broadcast_to(coeff_ref[pl.ds(i, 1)], (pairs, cycles, 8 * pairs))
        wide = jnp.where(mask, wide, 0.0).reshape(pairs * cycles, 8 * pairs)
        wide = wide.astype(jnp.bfloat16).astype(jnp.float32)
        lower = column < limit_ref[part]
        leg = leg_ref[part].reshape(pairs * cycles, packed)
        beyond = [
            jnp.sum(wide * leg[:, at : at + 1].astype(jnp.float32), axis=0, keepdims=True)
            for at in range(whole, packed)
        ]
        beyond.append(jnp.zeros((8 - len(beyond), 8 * pairs), jnp.float32))
        wide = jnp.concatenate([wide] + beyond, axis=0).T
        beyond = wide[half:, pairs * cycles : pairs * cycles + packed - whole].astype(jnp.bfloat16)
        wide = wide[:, : pairs * cycles].astype(jnp.bfloat16)
        left = jnp.dot(wide[:half], leg[:, :split], preferred_element_type=jnp.float32)
        right = jnp.dot(wide, leg[:, split:whole], preferred_element_type=jnp.float32)
        for s in range(2):
            for f in range(FIELDS):
                at = (s * FIELDS + f) * pairs
                out_vmem[s, f, 0, part, :split] = left[at : at + pairs].astype(jnp.bfloat16)
                low, high = right[at : at + pairs], right[half + at : half + at + pairs]
                out_vmem[s, f, 0, part, split:whole] = jnp.where(lower, low, high).astype(jnp.bfloat16)
                out_vmem[s, f, 0, part, whole:] = beyond[at : at + pairs]
        write(i).start()

    for i in range(blocks):
        write(i).wait()


def grid_kernel(
    points_dev, levs, split, length_hbm, weight_hbm, low_hbm, forcing_hbm, mixing_hbm, spec_hbm, leg_hbm,
    out_ref, limit_ref, leg_ref,
    length_ref, weight_ref, low_ref, forcing_ref, mixing_ref,
    cos_tab, sin_tab, cos_out, sin_out, grid_ref, force_ref,
    outgoing, incoming, partial, arrived, spec_vmem, four_ref, wave_ref,
    send_sem, recv_sem, send_back, recv_back, leg_sem, spec_sem, small_sem,
):
    blocks, cycles, wide = four_ref.shape
    pairs = wide // 8
    packed = leg_ref.shape[2]
    each = wide // 4

    def read_spec(i):
        part = pl.ds(pl.multiple_of(i * pairs, pairs), pairs)
        return pltpu.make_async_copy(
            spec_hbm.at[:, :, :, part], spec_vmem.at[:, :, :, part], spec_sem.at[i]
        )

    def read_leg(i):
        part = pl.ds(pl.multiple_of(i * pairs, pairs), pairs)
        return pltpu.make_async_copy(leg_hbm.at[part], leg_ref.at[part], leg_sem.at[i])

    small = [
        pltpu.make_async_copy(src, dst, small_sem.at[k])
        for k, (src, dst) in enumerate(
            (
                (low_hbm, low_ref), (length_hbm, length_ref), (weight_hbm, weight_ref),
                (forcing_hbm, forcing_ref), (mixing_hbm, mixing_ref),
            )
        )
    ]
    for copy in small[:3]:
        copy.start()

    rows = FIELDS * levs
    outer = cos_out.shape[0]
    used = pl.cdiv(points_dev, INNER)
    slots, _, lanes = incoming.shape
    bands = slots // levs
    band_id = lax.axis_index("band")
    lev_id = lax.axis_index("lev")
    me = band_id * levs + lev_id
    base = lev_id * points_dev
    barrier = pltpu.get_barrier_semaphore()

    def each_peer(act, midway=None):
        def of_band(flips, skip):
            band = toggled(band_id, flips, bands)
            for turn in range(levs - 1, skip - 1, -1):
                act(band, (lev_id + turn) % levs)

        if slots <= 64:
            for flips in range(bands - 1, 0, -1):
                of_band(flips, 0)
                if midway and flips == bands - 2:
                    midway()
        else:
            @pl.loop(1, bands)
            def _(step):
                of_band(bands - step, 0)

            if midway:
                midway()
        of_band(0, 1)

    def read_all():
        for i in range(blocks):
            read_spec(i).start()
            read_leg(i).start()
        for copy in small[3:]:
            copy.start()

    each_peer(
        lambda band, lev: pl.semaphore_signal(
            barrier, inc=1, device_id={"band": band, "lev": lev}, device_id_type=pl.DeviceIdType.MESH
        ),
        read_all,
    )

    for at, copy in enumerate(small[:3]):
        copy.wait()
    length = length_ref[band_id]
    inverse_length = 1.0 / jnp.full((1, lanes), length, jnp.int32).astype(jnp.float32)
    factor = inverse_length * weight_ref[band_id]

    own = blocks * pairs
    line = low_ref[...].reshape(1, bands * own)
    low = jnp.concatenate([line[:, k * own : (k + 1) * own] for k in range(bands)], axis=0)
    parts = [low, TRUNC - low]
    if lanes > blocks * each:
        parts.append(jnp.full((bands, lanes - blocks * each), 1 << 14, jnp.int32))
    wave_ref[...] = jnp.concatenate(parts, axis=1)
    mine = jnp.broadcast_to(wave_ref[pl.ds(band_id, 1), :].astype(jnp.float32), (8, lanes)).T
    limit_ref[...] = TRUNC + 1 - mine[: blocks * pairs, 0:1].astype(jnp.int32)

    twice, inverse_twice = 2 * length, 0.5 * inverse_length

    def tables(c):
        span = pl.ds(pl.multiple_of(c * lanes, lanes), lanes)
        wave = wave_ref[pl.ds(c, 1), :]
        eight = lax.broadcasted_iota(jnp.int32, (8, lanes), 0)
        c0, s0 = sincos(wave, eight * 2 + 1, twice, inverse_twice)
        c1, s1 = sincos(wave, eight * 16, twice, inverse_twice)
        c2, s2 = sincos(wave, eight * 128, twice, inverse_twice)
        steps = lax.broadcasted_iota(jnp.int32, (outer, lanes), 0)
        c3, s3 = sincos(wave, 2 * base + INNER - 1 + steps * (2 * INNER), twice, inverse_twice)
        cos_out[:, span] = c3
        sin_out[:, span] = s3
        for high in range(HALF // 64):
            ch, sh = c2[high : high + 1], s2[high : high + 1]
            cj, sj = ch * c1 - sh * s1, ch * s1 + sh * c1
            for mid in range(8):
                cm, sm = cj[mid : mid + 1], sj[mid : mid + 1]
                at = high * 64 + mid * 8
                cos_tab[at : at + 8, span] = (c0 * cm - s0 * sm).astype(jnp.bfloat16)
                sin_tab[at : at + 8, span] = (s0 * cm + c0 * sm).astype(jnp.bfloat16)

    mask = diagonal(pairs, cycles)
    column = split + lax.broadcasted_iota(jnp.int32, (pairs, packed - split), 1)
    inner = (((1,), (1,)), ((), ()))

    def legendre(i):
        part = pl.ds(pl.multiple_of(i * pairs, pairs), pairs)
        lower = column < limit_ref[part]
        whole, lows, highs = [], [], []
        for s in range(2):
            for f in range(FIELDS):
                whole.append(spec_vmem[s, f, 0, part, :split])
                row = spec_vmem[s, f, 0, part, split:].astype(jnp.float32)
                lows.append(jnp.where(lower, row, 0.0))
                highs.append(jnp.where(lower, 0.0, row))
        left = jnp.concatenate(whole, axis=0)
        right = jnp.concatenate(lows + highs, axis=0).astype(jnp.bfloat16)
        leg = leg_ref[part].reshape(pairs * cycles, packed)
        full = lax.dot_general(leg[:, split:], right, inner, preferred_element_type=jnp.float32)
        some = lax.dot_general(leg[:, :split], left, inner, preferred_element_type=jnp.float32)
        full = full + jnp.concatenate([some, jnp.zeros_like(some)], axis=1)
        full = full.reshape(pairs, cycles, 8 * pairs)
        four_ref[i] = jnp.sum(jnp.where(mask, full, 0.0), axis=0)

    def arrive(i):
        read_spec(i).wait()
        read_leg(i).wait()

    group = 2 if blocks % 2 == 0 else 1
    early = min(2, bands)

    pl.loop(0, early)(tables)

    @pl.loop(0, blocks // group)
    def _(step):
        first = step * group
        for at in range(group):
            arrive(first + at)
        for at in range(group):
            legendre(first + at)

    sides = []
    for k in range(4):
        parts = [
            four_ref[i, :, (4 * h + k) * pairs : (4 * h + k + 1) * pairs]
            for h in range(2)
            for i in range(blocks)
        ]
        if lanes > blocks * each:
            parts.append(jnp.zeros((cycles, lanes - blocks * each), jnp.float32))
        sides.append(jnp.concatenate(parts, axis=1))
    for j in range(cycles):
        block = jnp.concatenate([side[j : j + 1] for side in sides], axis=0)
        outgoing[j] = block.astype(jnp.bfloat16)

    pl.semaphore_wait(barrier, slots - 1)

    def send(source, target, here, there):
        def act(band, lev):
            pltpu.make_async_remote_copy(
                src_ref=source(band, lev), dst_ref=target.at[me], send_sem=here,
                recv_sem=there, device_id={"band": band, "lev": lev},
                device_id_type=pl.DeviceIdType.MESH,
            ).start()
        return act

    each_peer(send(lambda band, lev: outgoing.at[band], incoming, send_sem, recv_sem.at[band_id]))
    incoming[me] = outgoing[band_id]

    pl.loop(early, bands)(tables)

    def force_at(start):
        stop = min(start + HALF, points_dev)
        if stop <= start:
            return jnp.zeros((rows, HALF), jnp.float32)
        force = [forcing_ref[f, :, start:stop].astype(jnp.float32) for f in range(FIELDS)]
        force = jnp.concatenate(force, axis=0)
        if stop < start + HALF:
            rest = jnp.zeros((rows, start + HALF - stop), jnp.float32)
            force = jnp.concatenate([force, rest], axis=1)
        return force

    for copy in small[3:]:
        copy.wait()
    before = jnp.concatenate([force_at(a * INNER) for a in range(used)], axis=0)
    turned = lax.broadcasted_iota(jnp.int32, (HALF, HALF), 0) + lax.broadcasted_iota(
        jnp.int32, (HALF, HALF), 1
    )
    turned = jnp.where(turned == HALF - 1, 1.0, 0.0).astype(jnp.bfloat16)
    force_ref[0] = jnp.concatenate([force_at(a * INNER + HALF) for a in range(used)], axis=0)
    force_ref[1] = jnp.dot(before.astype(jnp.bfloat16), turned, preferred_element_type=jnp.float32)

    def wait_all(semaphore, buffer, count):
        most = buffer.at[pl.ds(0, count)]
        pltpu.make_async_copy(most, most, semaphore).wait()

    contract = (((1,), (1,)), ((), ()))
    near = 2 if bands % 2 == 0 else 1
    groups = bands // near

    def span_of(group):
        return pl.ds(pl.multiple_of(group * (near * lanes), near * lanes), near * lanes)

    def waves_of(group):
        return jnp.concatenate([wave_ref[pl.ds(group * near + at, 1), :] for at in range(near)], axis=1)

    def synthesis(group):
        span, wave = span_of(group), waves_of(group)
        gain = jnp.where(wave == 0, 1.0, 2.0)
        live = 2 * wave < length
        cells = [
            jnp.concatenate([incoming[(group * near + at) * levs + lev] for at in range(near)], axis=1)
            for lev in range(levs)
        ]
        cells = [cell.astype(jnp.float32) for cell in cells]
        order = [(f, lev) for f in range(FIELDS) for lev in range(levs)]
        re = jnp.concatenate([cells[lev][f : f + 1] for f, lev in order], axis=0)
        im = jnp.concatenate([cells[lev][FIELDS + f : FIELDS + f + 1] for f, lev in order], axis=0)
        re = jnp.where(live, re * gain, 0.0)
        im = jnp.where(live, im * -gain, 0.0)
        twist_re, twist_im = [], []
        for a in range(used):
            co, so = cos_out[a : a + 1, span], sin_out[a : a + 1, span]
            twist_re.append(re * co + im * so)
            twist_im.append(im * co - re * so)
        twist_re = jnp.concatenate(twist_re, axis=0).astype(jnp.bfloat16)
        twist_im = jnp.concatenate(twist_im, axis=0).astype(jnp.bfloat16)
        even = lax.dot_general(twist_re, cos_tab[:, span], contract, preferred_element_type=jnp.float32)
        odd = lax.dot_general(twist_im, sin_tab[:, span], contract, preferred_element_type=jnp.float32)
        return even, odd

    def wait_group(flips, own):
        group = toggled(band_id // near, flips, groups)
        for at in range(near):
            if own:
                first = (band_id + at) % near
                wait_all(recv_sem.at[group * near + first], incoming, levs - (at == 0))
            else:
                wait_all(recv_sem.at[group * near + at], incoming, levs)
        return group

    if groups <= 8:
        even, odd = 0.0, 0.0
        for last in range(groups - 1, -1, -STEP):
            these = range(last, max(last - STEP, -1), -1)
            these = [wait_group(flips, flips == 0) for flips in these]
            for group in these:
                half = synthesis(group)
                even, odd = even + half[0], odd + half[1]
    else:
        grid_ref[0], grid_ref[1] = synthesis(wait_group(0, True))

        @pl.loop(1, groups)
        def _(flips):
            half = synthesis(wait_group(flips, False))
            grid_ref[0] += half[0]
            grid_ref[1] += half[1]

        even, odd = grid_ref[0], grid_ref[1]

    lane = lax.broadcasted_iota(jnp.int32, (rows, HALF), 1)
    mixing = jnp.concatenate([mixing_ref[f].astype(jnp.float32) for f in range(FIELDS)], axis=0)

    def physics(side, values, a):
        point = a * INNER + (HALF - 1 - lane if side else HALF + lane)
        inside = (point < points_dev) & (base + point < length)
        cell = jnp.where(inside, values, 0.0)
        product = (cell[:levs] * cell[levs:]).astype(jnp.bfloat16).astype(jnp.float32)
        total = cell + force_ref[side, a * rows : (a + 1) * rows]
        for l2 in range(levs):
            total = total + mixing[:, l2 : l2 + 1] * product[l2 : l2 + 1]
        return jnp.where(inside, total, 0.0)

    sums, gaps = [], []
    for a in range(used):
        at = slice(a * rows, (a + 1) * rows)
        after, before = physics(0, even[at] + odd[at], a), physics(1, even[at] - odd[at], a)
        sums.append(after + before)
        gaps.append(after - before)
    sums = jnp.concatenate(sums, axis=0).astype(jnp.bfloat16)
    gaps = jnp.concatenate(gaps, axis=0).astype(jnp.bfloat16)

    send_partial = send(
        lambda band, lev: partial.at[band * levs + lev], arrived, send_back, recv_back
    )

    def analysis(band):
        pieces = []
        for start in range(0, lanes, CHUNK):
            size = min(CHUNK, lanes - start)
            span = pl.ds(pl.multiple_of(band * lanes + start, 128), size)
            cos_part = jnp.dot(sums, cos_tab[:, span], preferred_element_type=jnp.float32)
            sin_part = jnp.dot(gaps, sin_tab[:, span], preferred_element_type=jnp.float32)
            re = jnp.zeros((rows, size), jnp.float32)
            im = jnp.zeros((rows, size), jnp.float32)
            for a in range(used):
                co, so = cos_out[a : a + 1, span], sin_out[a : a + 1, span]
                cp, sp = cos_part[a * rows : (a + 1) * rows], sin_part[a * rows : (a + 1) * rows]
                re = re + (cp * co - sp * so)
                im = im + (cp * so + sp * co)
            pieces.append((re, im))
        re, im = (jnp.concatenate(side, axis=1) for side in zip(*pieces))
        keep = 2 * wave_ref[pl.ds(band, 1), :] < length
        re = jnp.where(keep, re * factor, 0.0)
        im = jnp.where(keep, im * -factor, 0.0)
        for lev in range(levs):
            picks = [side[f * levs + lev : f * levs + lev + 1] for side in (re, im) for f in range(FIELDS)]
            partial[band * levs + lev] = jnp.concatenate(picks, axis=0).astype(jnp.bfloat16)

    def serve(band):
        analysis(band)
        for lev in range(levs):
            pl.when((band != band_id) | (lev != lev_id))(functools.partial(send_partial, band, lev))

    if bands <= 8:
        for band in range(bands):
            serve(band)
    else:
        pl.loop(0, bands)(serve)
    arrived[me] = partial[me]

    wait_all(recv_back, arrived, slots - 1)
    levels_sum = []
    for j in range(cycles):
        total = arrived[j * levs].astype(jnp.float32)
        for lev in range(1, levs):
            total = total + arrived[j * levs + lev].astype(jnp.float32)
        levels_sum.append(total)
    for k in range(4):
        side = jnp.concatenate([total[k : k + 1] for total in levels_sum], axis=0)
        for h in range(2):
            for i in range(blocks):
                at, lane = (4 * h + k) * pairs, (h * blocks + i) * pairs
                out_ref[i, :, at : at + pairs] = side[:, lane : lane + pairs]
    wait_all(send_sem, incoming, slots - 1)
    wait_all(send_back, arrived, slots - 1)


def on_device(spectral, legendre, cycle_len, pair_wave, quad_weight, forcing, mixing):
    band_count = lax.axis_size("band")
    lev_count = lax.axis_size("lev")
    pair_dev = spectral.shape[3]
    cycles = legendre.shape[1]
    levels, points_dev = forcing.shape[1], forcing.shape[3]
    rows = FIELDS * levels
    pairs = pair_block(pair_dev)
    blocks = pair_dev // pairs

    each_band = pl.cdiv(2 * pair_dev, 128) * 128
    waves = band_count * each_band
    used = pl.cdiv(points_dev, INNER)
    outer = pl.cdiv(used, 8) * 8
    force = forcing.reshape(FIELDS, levels, points_dev)
    vmem = pl.BlockSpec(memory_space=pltpu.VMEM)
    slots = band_count * lev_count
    message = pltpu.VMEM((slots, 2 * FIELDS, each_band), jnp.bfloat16)
    split = (TRUNC + 2 - pair_wave.shape[0]) // 128 * 128
    hbm = pl.BlockSpec(memory_space=pltpu.HBM)
    coeff, limit, leg = pl.pallas_call(
        functools.partial(grid_kernel, points_dev, lev_count, split),
        in_specs=[hbm] * 7,
        out_specs=[vmem] * 3,
        out_shape=[
            pltpu.VMEM((blocks, cycles, 8 * pairs), jnp.float32),
            pltpu.VMEM((pair_dev, 1), jnp.int32),
            pltpu.VMEM(legendre.shape, jnp.bfloat16),
        ],
        scratch_shapes=[
            pltpu.SMEM(cycle_len.shape, jnp.int32),
            pltpu.SMEM(quad_weight.shape, jnp.float32),
            pltpu.VMEM(pair_wave.shape, jnp.int32),
            pltpu.VMEM(force.shape, jnp.bfloat16),
            pltpu.VMEM(mixing.shape, jnp.bfloat16),
            pltpu.VMEM((HALF, waves), jnp.bfloat16),
            pltpu.VMEM((HALF, waves), jnp.bfloat16),
            pltpu.VMEM((outer, waves), jnp.float32),
            pltpu.VMEM((outer, waves), jnp.float32),
            pltpu.VMEM((2, used * rows, HALF), jnp.float32),
            pltpu.VMEM((2, used * rows, HALF), jnp.float32),
            pltpu.VMEM((cycles, 2 * FIELDS, each_band), jnp.bfloat16),
            message, message, message,
            pltpu.VMEM(spectral.shape, jnp.bfloat16),
            pltpu.VMEM((blocks, cycles, 8 * pairs), jnp.float32),
            pltpu.VMEM((band_count, each_band), jnp.int32),
            pltpu.SemaphoreType.DMA,
            pltpu.SemaphoreType.DMA((band_count,)),
            pltpu.SemaphoreType.DMA,
            pltpu.SemaphoreType.DMA,
            pltpu.SemaphoreType.DMA((blocks,)),
            pltpu.SemaphoreType.DMA((blocks,)),
            pltpu.SemaphoreType.DMA((5,)),
        ],
        compiler_params=pltpu.CompilerParams(
            collective_id=0, has_side_effects=True, vmem_limit_bytes=VMEM_LIMIT
        ),
    )(
        *(
            pltpu.with_memory_space_constraint(array, pltpu.HBM)
            for array in (cycle_len, quad_weight, pair_wave, force, mixing, spectral, legendre)
        )
    )
    return pl.pallas_call(
        functools.partial(direct_kernel, split),
        in_specs=[vmem, vmem, vmem],
        out_specs=hbm,
        out_shape=jax.ShapeDtypeStruct(spectral.shape, jnp.bfloat16),
        scratch_shapes=[pltpu.VMEM(spectral.shape, jnp.bfloat16), pltpu.SemaphoreType.DMA((blocks,))],
        compiler_params=pltpu.CompilerParams(vmem_limit_bytes=VMEM_LIMIT),
    )(limit, coeff, leg)


def solution(mesh):
    return jax.shard_map(
        on_device,
        mesh=mesh,
        in_specs=(
            P(None, None, "lev", "band", None),
            P("band", None, None),
            P(),
            P(),
            P(),
            P(None, None, "band", "lev"),
            P(),
        ),
        out_specs=P(None, None, "lev", "band", None),
        check_vma=False,
    )
```
